256 devices in a mesh: docs: 128 (over y, z_lo, x, core), pb: 2 (over z_hi).
Axes of the slice: x: 4, y: 4, z: 8 (z_hi: 2, z_lo: 4; z = z_hi * 4 + z_lo), core: 2. Of those that a mesh axis runs over, the one named last changes fastest.
Arguments:
- queries: bfloat16 [1024, 32, 128], P('docs', 'pb'), may hold values from -0.1875 to 0.1875
- documents: bfloat16 [16384, 64, 128], P('docs'), may hold values from -1.75 to 1.75
- lengths: int32 [16384], P('docs'), may hold values from 1 to 64
- pattern: int32 [8, 128], replicated, may hold values from 0 to 1
Outputs:
- scores: float32 [128, 8, 16384], P(None, 'pb', 'docs')
The draws below stay inside these ranges and needn't reach their ends.
All inputs are finite; a program needn't handle non-finite values.
Results may differ from the reference program's by a relative error of at most 0.0003.
Values may be sent and summed in bfloat16 or wider, within the bound.
A program may use at most 64 MiB of HBM per device.

```python
import jax
import jax.numpy as jnp
from jax import lax

DIM = 128
QTOK = 32
DTOK = 64
BLOCK = 128
QBLK = 8
NQ = 1024
QROW = 8
DBLK = 128
NDOC = 16384


def draw_pattern(key, part):
    level_key, roll_key = jax.random.split(key)
    levels = jax.random.randint(level_key, (1, DBLK), 0, 5)
    dice_rolls = jax.random.randint(roll_key, (QBLK, DBLK), 0, 16)
    return (dice_rolls < levels).astype(jnp.int32)


def touch_ends(entries, stream_key, low, high):
    longest = entries.shape.index(max(entries.shape))
    spots = []
    for shift in (0, 1):
        where = [jax.random.randint(jax.random.fold_in(stream_key, axis), (), 0, length) for axis, length in enumerate(entries.shape)]
        where[longest] = (where[longest] + shift) % entries.shape[longest]
        spots.append(tuple(where))
    return entries.at[spots[0]].set(low).at[spots[1]].set(high)


def block_scale(rng, extent, shards, low, top_value):
    def one(dim, blocks):
        steps = jax.random.uniform(jax.random.fold_in(jax.random.fold_in(rng, 6), dim), (blocks,), jnp.float32, low / len(shards), top_value / len(shards))
        return jnp.repeat(jnp.exp(steps), extent[dim] // blocks).reshape((-1,) + (1,) * (len(extent) - dim - 1))

    loudness = one(*shards[0])
    for cut in shards[1:]:
        loudness = loudness * one(*cut)
    return loudness


def scatter_about(stream_key, shape, scale, bound, cuts=(), kind=jnp.bfloat16):
    array = scale * jax.random.normal(stream_key, shape, jnp.float32)
    if cuts:
        array = array * block_scale(stream_key, shape, cuts, -0.22, 0.18)
    return jnp.clip(array, -bound, bound).astype(kind)


def setup_inputs(seed: int = 0) -> dict:
    streams_of = jax.random.split(jax.random.key(seed), 5)
    queries = scatter_about(streams_of[0], (NQ, QTOK, DIM), 0.03, 0.1875, ((0, 128), (1, 2)))
    documents = scatter_about(streams_of[1], (NDOC, DTOK, DIM), 0.3, 1.75, ((0, 128),))
    lengths = touch_ends(jax.random.randint(streams_of[2], (NDOC,), 1, DTOK + 1), jax.random.fold_in(streams_of[2], 1), 1, DTOK).astype(jnp.int32)
    pattern = draw_pattern(jax.random.fold_in(streams_of[4], 71), 0)
    return {"queries": queries, "documents": documents, "lengths": lengths, "pattern": pattern}


def block_scores(query_block, doc_block, doc_lengths):
    qcount, tcount, width_dim = query_block.shape
    dcount, dtokens, _ = doc_block.shape
    group_size = min(16, dcount)
    doc_groups = doc_block.reshape(dcount // group_size, group_size * dtokens, width_dim)
    len_groups = doc_lengths.reshape(dcount // group_size, group_size)
    positions = jnp.arange(dtokens, dtype=jnp.int32)
    query_wide = query_block.astype(jnp.float32)

    def one_group(operands):
        doc_rows, limits = operands
        similar = jnp.einsum('qtc,gc->qtg', query_wide, doc_rows.astype(jnp.float32))
        is_valid = (positions[None, :] < limits[:, None]).reshape(group_size * dtokens)
        similar = jnp.where(is_valid[None, None, :], similar, -1e30)
        maxima = jnp.max(similar.reshape(qcount, tcount, group_size, dtokens), axis=3)
        return jnp.sum(maxima, axis=1)

    pieces = lax.map(one_group, (doc_groups, len_groups))
    return jnp.transpose(pieces, (1, 0, 2)).reshape(qcount, dcount)


def reference(queries, documents, lengths, pattern):
    query_blocks = queries.reshape(QBLK, BLOCK, QTOK, DIM)
    doc_blocks = documents.reshape(DBLK, BLOCK, DTOK, DIM)
    len_blocks = lengths.reshape(DBLK, BLOCK)

    def per_query(operands):
        query_block, flag_row = operands

        def per_doc(inner):
            doc_block, doc_lengths, flag = inner

            def active():
                return block_scores(query_block, doc_block, doc_lengths)

            def empty():
                return jnp.zeros((BLOCK, BLOCK), jnp.float32)

            return lax.cond(flag > 0, active, empty)

        return lax.map(per_doc, (doc_blocks, len_blocks, flag_row))

    result = lax.map(per_query, (query_blocks, pattern))
    return jnp.transpose(result, (0, 2, 1, 3)).reshape(NQ // QROW, QROW, NDOC)
```

```python
import functools

import jax
import jax.numpy as jnp
from jax import lax
from jax.experimental import pallas as pl
from jax.experimental.pallas import tpu as pltpu
from jax.sharding import PartitionSpec as P

MESH = pl.DeviceIdType.MESH


def gather_kernel(q_ref, out_ref, tmp, prep, zs, zr, ss, sr, ds_, dr, lsem):
    idx = lax.axis_index("docs")
    zh = lax.axis_index("pb")
    c = idx % 2
    x = (idx // 2) % 4
    zl = (idx // 8) % 4
    y = idx // 32
    z = zh * 4 + zl

    def dev(y, zl, x, c, h):
        return {"docs": ((y * 4 + zl) * 4 + x) * 2 + c, "pb": h}

    xp, xm, yp, ym = (x + 1) % 4, (x + 3) % 4, (y + 1) % 4, (y + 3) % 4
    x2, y2 = (x + 2) % 4, (y + 2) % 4
    right, left = dev(y, zl, xp, c, zh), dev(y, zl, xm, c, zh)
    up, down = dev(yp, zl, x, c, zh), dev(ym, zl, x, c, zh)
    twin = dev(y, zl, x, 1 - c, zh)
    column = []
    for s in range(1, 8):
        zt = (z + s) % 8
        column.append((zt // 4, dev(y, zt % 4, x, c, zt // 4)))

    barrier = pltpu.get_barrier_semaphore()
    for d in [right, left, up, down, twin] + [d for _, d in column]:
        pl.semaphore_signal(barrier, inc=1, device_id=d, device_id_type=MESH)

    for h in range(2):
        for q in range(4):
            tmp[pl.ds(q, 16, stride=4), :] = q_ref[4 * h + q].astype(jnp.float32)
        prep[h] = tmp[...].astype(jnp.bfloat16)

    pl.semaphore_wait(barrier, 12)

    def send(src, s_sem, r_sem, d):
        cp = pltpu.make_async_remote_copy(
            src_ref=src, dst_ref=src, send_sem=s_sem, recv_sem=r_sem, device_id=d, device_id_type=MESH)
        cp.start()
        return cp

    own = out_ref.at[y, zl, x, c, zh]
    first = []
    for s, (ht, d) in enumerate(column):
        cp = pltpu.make_async_remote_copy(
            src_ref=prep.at[ht], dst_ref=own, send_sem=zs.at[s], recv_sem=zr.at[s], device_id=d, device_id_type=MESH)
        cp.start()
        first.append(cp)
    lc = pltpu.make_async_copy(prep.at[zh], own, lsem)
    lc.start()
    lc.wait()
    for cp in first:
        cp.wait_recv()

    sent = list(first)
    mine = [0]
    twins = []

    def share(ref):
        k = len(twins)
        twins.append(send(ref, ds_.at[k], dr.at[k], twin))

    a = pl.ds(0, 2)
    b = pl.ds(2, 2)
    pa = out_ref.at[y, a, x, c]
    pb = out_ref.at[y, b, x, c]
    s0 = send(pa, ss.at[0], sr.at[0], right)
    s1 = send(pa, ss.at[1], sr.at[1], left)
    s2 = send(pb, ss.at[2], sr.at[2], up)
    s3 = send(pb, ss.at[3], sr.at[3], down)
    share(out_ref.at[y, :, x, c])
    s0.wait_recv()
    s4 = send(out_ref.at[y, 0, xm, c], ss.at[4], sr.at[4], right)
    s1.wait_recv()
    s5 = send(out_ref.at[y, 1, xp, c], ss.at[5], sr.at[5], left)
    s2.wait_recv()
    s6 = send(out_ref.at[ym, 2, x, c], ss.at[6], sr.at[6], up)
    s3.wait_recv()
    s7 = send(out_ref.at[yp, 3, x, c], ss.at[7], sr.at[7], down)
    share(out_ref.at[y, a, xm, c])
    share(out_ref.at[y, a, xp, c])
    share(out_ref.at[ym, b, x, c])
    share(out_ref.at[yp, b, x, c])
    s4.wait_recv()
    s5.wait_recv()
    t0 = send(out_ref.at[y, a, :, c], ss.at[8], sr.at[8], up)
    t1 = send(out_ref.at[y, a, :, c], ss.at[9], sr.at[9], down)
    s6.wait_recv()
    s7.wait_recv()
    t2 = send(out_ref.at[:, b, x, c], ss.at[10], sr.at[10], right)
    t3 = send(out_ref.at[:, b, x, c], ss.at[11], sr.at[11], left)
    share(out_ref.at[y, a, x2, c])
    share(out_ref.at[y2, b, x, c])
    t0.wait_recv()
    t4 = send(out_ref.at[ym, 0, :, c], ss.at[12], sr.at[12], up)
    share(out_ref.at[ym, a, :, c])
    t1.wait_recv()
    t5 = send(out_ref.at[yp, 1, :, c], ss.at[13], sr.at[13], down)
    share(out_ref.at[yp, a, :, c])
    t2.wait_recv()
    t6 = send(out_ref.at[:, 2, xm, c], ss.at[14], sr.at[14], right)
    share(out_ref.at[:, b, xm, c])
    t3.wait_recv()
    t7 = send(out_ref.at[:, 3, xp, c], ss.at[15], sr.at[15], left)
    share(out_ref.at[:, b, xp, c])
    t4.wait_recv()
    share(out_ref.at[y2, 0, :, c])
    t5.wait_recv()
    share(out_ref.at[y2, 1, :, c])
    t6.wait_recv()
    share(out_ref.at[:, 2, x2, c])
    t7.wait_recv()
    share(out_ref.at[:, 3, x2, c])
    for cp in twins:
        cp.wait_recv()
    for cp in first + [s0, s1, s2, s3, s4, s5, s6, s7, t0, t1, t2, t3, t4, t5, t6, t7] + twins:
        cp.wait_send()


def gather(queries):
    return pl.pallas_call(
        gather_kernel,
        name="gather_queries",
        out_shape=jax.ShapeDtypeStruct((4, 4, 4, 2, 2, 64, 128), jnp.bfloat16),
        in_specs=[pl.BlockSpec(memory_space=pltpu.VMEM)],
        out_specs=pl.BlockSpec(memory_space=pl.ANY),
        scratch_shapes=[
            pltpu.VMEM((64, 128), jnp.float32),
            pltpu.VMEM((2, 64, 128), jnp.bfloat16),
            pltpu.SemaphoreType.DMA((7,)),
            pltpu.SemaphoreType.DMA((7,)),
            pltpu.SemaphoreType.DMA((16,)),
            pltpu.SemaphoreType.DMA((16,)),
            pltpu.SemaphoreType.DMA((15,)),
            pltpu.SemaphoreType.DMA((15,)),
            pltpu.SemaphoreType.DMA,
        ],
        compiler_params=pltpu.CompilerParams(collective_id=0, has_side_effects=True),
    )(queries)

CH = 64
NS = 8


def score_kernel(pos, pat_ref, len_ref, order_ref, rank_ref, q_hbm, d_ref, out_ref, *scratch):
    pl.run_scoped(
        functools.partial(score_body, pos, pat_ref, len_ref, order_ref, rank_ref, q_hbm, d_ref, out_ref, *scratch),
        *([pltpu.ACC(0)((CH, 256), jnp.float32)] * (2 * NS) + [pltpu.ACC(1)((CH, 256), jnp.float32)] * (2 * NS)),
    )


def score_body(pos, pat_ref, len_ref, order_ref, rank_ref, q_hbm, d_ref, out_ref,
               qbuf, dt, tmp, amax, total, chunks, blocks, sems, *accs):
    acc = (accs[:2 * NS], accs[2 * NS:])
    col = pos()

    def note(k, n):
        on = pat_ref[k, col] > 0

        @pl.when(on)
        def _():
            blocks[n] = k
            pltpu.make_async_copy(q_hbm.at[k], qbuf.at[k], sems.at[k]).start()

        return n + on.astype(jnp.int32)

    count = lax.fori_loop(0, 8, note, 0)
    out_ref[...] = jnp.zeros_like(out_ref)

    @pl.when(count > 0)
    def _():
        def arrange(g, t):
            for i in range(8):
                d = order_ref[g * 8 + i]
                rows = d_ref[d].astype(jnp.float32)
                slot = lax.broadcasted_iota(jnp.int32, rows.shape, 0)
                tmp[pl.ds(i, 64, stride=8), :] = jnp.where(slot < len_ref[d], rows, rows[0:1])
            for i in range(8):
                dt[g * 8 + i] = tmp[i * CH:(i + 1) * CH].astype(jnp.bfloat16)
            need = (len_ref[order_ref[g * 8]] + 7) // 8

            def put(i, t):
                chunks[t] = g * 8 + i
                return t + 1

            return lax.fori_loop(0, need, put, t)

        t = lax.fori_loop(0, 16, arrange, 0)
        for i in range(NS):
            chunks[t + i] = chunks[t - 1]
        steps = (t + NS - 1) // NS
        units = count * 4
        total[...] = jnp.zeros_like(total)
        amax[...] = jnp.full_like(amax, -jnp.inf)

        def weights(u):
            k = blocks[u // 4]
            j = (u % 4) * 32

            @pl.when(u % 4 == 0)
            def _():
                pltpu.make_async_copy(q_hbm.at[k], qbuf.at[k], sems.at[k]).wait()

            for m in range(2):
                w = qbuf[k, :, pl.ds(pl.multiple_of(j + 16 * m, 16), 16), :].reshape(256, 128)
                pltpu.matmul_push_rhs(jnp.concatenate([w, jnp.zeros_like(w)], axis=1), 0, m, transpose=True)

        def lhs(step, s):
            w = dt[chunks[step * NS + s]]
            return jnp.concatenate([w, jnp.zeros_like(w)], axis=1)

        def pop(step, p, s):
            g = chunks[step * NS + s] // 8
            for m in range(2):
                r = pltpu.matmul_pop(acc[m][p * NS + s])
                r = jnp.max(r.reshape(8, 8, 256), axis=0)
                amax[g, m] = jnp.maximum(amax[g, m], r)

        def close(u):
            k = jnp.where(u < 0, 8, blocks[jnp.maximum(u, 0) // 4])
            total[k] += amax[:, 0] + amax[:, 1]
            amax[...] = jnp.full_like(amax, -jnp.inf)

        def half(p, state):
            u, m, u1, m1, u2, m2, u3 = state

            @pl.when(u2 != u3)
            def _():
                close(u3)

            pop(m2, p, 0)
            x = lhs(m, 0)
            head = (m == 0) & (u1 != u)

            @pl.when(head)
            def _():
                for k in range(2):
                    pltpu.matmul_acc_lhs(acc[k][p * NS], x, load_staged_rhs=0)

                @pl.when(u + 1 < units)
                def _():
                    weights(u + 1)

            @pl.when(jnp.logical_not(head))
            def _():
                for k in range(2):
                    pltpu.matmul_acc_lhs(acc[k][p * NS], x)

            for s in range(1, NS):
                pop(m2, p, s)
                x = lhs(m, s)
                for k in range(2):
                    pltpu.matmul_acc_lhs(acc[k][p * NS + s], x)
            last = m + 1 == steps
            end = last & (u + 1 == units)
            un = jnp.where(last & (u + 1 < units), u + 1, u)
            mn = jnp.where(end, m, jnp.where(last, 0, m + 1))
            return un, mn, u, m, u1, m1, u2

        weights(0)

        def both(i, state):
            return half(1, half(0, state))

        n = (units * steps + 1) // 2
        zero = jnp.int32(0)
        state = lax.fori_loop(0, n, both, (zero, zero, zero - 1, zero, zero - 1, zero, zero - 1))
        u, m, u1, m1, u2, m2, u3 = state
        for p in range(2):
            uu, mm, before = ((u2, m2, u3), (u1, m1, u2))[p]

            @pl.when(uu != before)
            def _():
                close(before)

            for s in range(NS):
                pop(mm, p, s)
        close(u1)

        rank = rank_ref[...]

        def finish(i, _):
            k = blocks[i]
            sums = total[k].reshape(128, 256)
            for part in range(2):
                turned = sums[:, part * 128:(part + 1) * 128].T.reshape(8, 2, 8, 128)
                folded = (turned[:, 0] + turned[:, 1])
                folded = folded[:, 0:4] + folded[:, 4:8]
                index = jnp.broadcast_to(rank.reshape(1, 1, 128), (8, 4, 128)).reshape(32, 128)
                out_ref[pl.ds(k * 16 + part * 8, 8)] = jnp.take_along_axis(
                    folded.reshape(32, 128), index, axis=1).reshape(8, 4, 128)
            return 0

        lax.fori_loop(0, count, finish, 0)


def score(pos, pattern, lengths, order, rank, rows, documents):
    smem = pl.BlockSpec(memory_space=pltpu.SMEM)
    vmem = pl.BlockSpec(memory_space=pltpu.VMEM)
    return pl.pallas_call(
        functools.partial(score_kernel, pos),
        name="score_blocks",
        out_shape=jax.ShapeDtypeStruct((128, 4, 128), jnp.float32),
        in_specs=[smem, smem, smem, vmem, pl.BlockSpec(memory_space=pltpu.HBM), vmem],
        out_specs=vmem,
        scratch_shapes=[
            pltpu.VMEM((8, 16, 128, 128), jnp.bfloat16),
            pltpu.VMEM((128, CH, 128), jnp.bfloat16),
            pltpu.VMEM((512, 128), jnp.float32),
            pltpu.VMEM((16, 2, 8, 256), jnp.float32),
            pltpu.VMEM((9, 16, 8, 256), jnp.float32),
            pltpu.SMEM((128 + NS,), jnp.int32),
            pltpu.SMEM((8,), jnp.int32),
            pltpu.SemaphoreType.DMA((8,)),
        ],
        compiler_params=pltpu.CompilerParams(vmem_limit_bytes=32 << 20),
    )(pattern, lengths, order, rank, rows, documents)


def ordering(lengths):
    e = jnp.arange(128, dtype=jnp.int32)
    ahead = (lengths[None, :] > lengths[:, None]) | ((lengths[None, :] == lengths[:, None]) & (e[None, :] < e[:, None]))
    rank = jnp.sum(ahead.astype(jnp.int32), axis=1)
    order = jnp.sum(jnp.where(rank[:, None] == e[None, :], e[:, None], 0), axis=0)
    return order, rank


def local(queries, documents, lengths, pattern):
    order, rank = ordering(lengths)
    rows = gather(queries).reshape(8, 16, 128, 128)
    return score(lambda: lax.axis_index("docs"), pattern, lengths, order, rank.reshape(1, 128), rows, documents)


def solution(mesh):
    return jax.shard_map(
        local,
        mesh=mesh,
        in_specs=(P("docs", "pb", None), P("docs", None, None), P("docs"), P()),
        out_specs=P(None, "pb", "docs"),
        check_vma=False,
    )
```

```python
import functools

import jax
import jax.numpy as jnp
from jax import lax
from jax.experimental import pallas as pl
from jax.experimental.pallas import tpu as pltpu
from jax.sharding import PartitionSpec as P

MESH = pl.DeviceIdType.MESH
CH = 64
NS = 8


def device(y, zl, x, c, h):
    return {"docs": ((y * 4 + zl) * 4 + x) * 2 + c, "pb": h}


def gather_kernel(q_ref, len_ref, d_hbm, q_out, dt_out, meta_out,
                  tmp, prep, docs, wide, dt, meta, meta_s, zs, zr, ss, sr, ts, tr, ls):
    idx = lax.axis_index("docs")
    zh = lax.axis_index("pb")
    c = idx % 2
    x = (idx // 2) % 4
    zl = (idx // 8) % 4
    y = idx // 32
    z = zh * 4 + zl
    xp, xm, yp, ym = (x + 1) % 4, (x + 3) % 4, (y + 1) % 4, (y + 3) % 4
    right, left = device(y, zl, xp, c, zh), device(y, zl, xm, c, zh)
    up, down = device(yp, zl, x, c, zh), device(ym, zl, x, c, zh)
    twin = device(y, zl, x, 1 - c, zh)
    column = []
    for s in range(1, 8):
        zt = (z + s) % 8
        column.append((zt // 4, device(y, zt % 4, x, c, zt // 4)))

    load = pltpu.make_async_copy(d_hbm, docs, ls.at[0])
    load.start()
    barrier = pltpu.get_barrier_semaphore()
    for d in [right, left, up, down, twin] + [d for _, d in column]:
        pl.semaphore_signal(barrier, inc=1, device_id=d, device_id_type=MESH)

    for h in range(2):
        for q in range(4):
            tmp[pl.ds(q, 16, stride=4), :] = q_ref[4 * h + q].astype(jnp.float32)
        prep[h] = tmp[...].astype(jnp.bfloat16)

    pl.semaphore_wait(barrier, 12)

    own = q_out.at[y, zl, x, zh]
    waits = []

    def send(src, dst, s_sem, r_sem, d):
        cp = pltpu.make_async_remote_copy(
            src_ref=src, dst_ref=dst, send_sem=s_sem, recv_sem=r_sem, device_id=d, device_id_type=MESH)
        cp.start()
        waits.append(cp)
        return cp

    first = [send(prep.at[ht], own, zs.at[s], zr.at[s], d) for s, (ht, d) in enumerate(column)]
    lc = pltpu.make_async_copy(prep.at[zh], own, ls.at[1])
    lc.start()

    lanes = jnp.broadcast_to(len_ref[...], (128, 128))
    cols = lanes.T
    r = lax.broadcasted_iota(jnp.int32, (128, 128), 0)
    k = lax.broadcasted_iota(jnp.int32, (128, 128), 1)
    ahead_col = (lanes > cols) | ((lanes == cols) & (k < r))
    ahead_row = (cols > lanes) | ((cols == lanes) & (r < k))
    rank_col = jnp.sum(jnp.where(ahead_col, 1, 0), axis=1, keepdims=True)
    rank_row = jnp.sum(jnp.where(ahead_row, 1, 0), axis=0, keepdims=True)
    here = rank_col == k
    meta[0:1] = jnp.sum(jnp.where(here, cols, 0), axis=0, keepdims=True)
    meta[1:2] = rank_row
    meta[2:3] = jnp.sum(jnp.where(here, r, 0), axis=0, keepdims=True)
    meta[3:8] = jnp.zeros((5, 128), jnp.int32)
    lm = pltpu.make_async_copy(meta, meta_s, ls.at[2])
    lm.start()
    lo = pltpu.make_async_copy(meta, meta_out.at[0], ls.at[3])
    lo.start()
    m0 = send(meta, meta_out.at[1], ts.at[0], tr.at[0], twin)
    lm.wait()
    load.wait()

    def arrange(g, _):
        for i in range(8):
            rows = docs[jnp.bitwise_and(meta_s[2, g * 8 + i], 127)].astype(jnp.float32)
            slot = lax.broadcasted_iota(jnp.int32, rows.shape, 0)
            wide[pl.ds(i, 64, stride=8), :] = jnp.where(slot < meta_s[0, g * 8 + i], rows, rows[0:1])
        for i in range(8):
            dt[g * 8 + i] = wide[i * CH:(i + 1) * CH].astype(jnp.bfloat16)
        return 0

    lax.fori_loop(0, 16, arrange, 0)
    ld = pltpu.make_async_copy(dt, dt_out.at[0], ls.at[4])
    ld.start()
    m1 = send(dt, dt_out.at[1], ts.at[1], tr.at[1], twin)

    lc.wait()
    for cp in first:
        cp.wait_recv()

    a = pl.ds(0, 2)
    b = pl.ds(2, 2)

    def pass_on(n, ref, d):
        return send(ref, ref, ss.at[n], sr.at[n], d)

    s0 = pass_on(0, q_out.at[y, a, x], right)
    s1 = pass_on(1, q_out.at[y, a, x], left)
    s2 = pass_on(2, q_out.at[y, b, x], up)
    s3 = pass_on(3, q_out.at[y, b, x], down)
    s0.wait_recv()
    s4 = pass_on(4, q_out.at[y, 0, xm], right)
    s1.wait_recv()
    s5 = pass_on(5, q_out.at[y, 1, xp], left)
    s2.wait_recv()
    s6 = pass_on(6, q_out.at[ym, 2, x], up)
    s3.wait_recv()
    s7 = pass_on(7, q_out.at[yp, 3, x], down)
    s4.wait_recv()
    s5.wait_recv()
    t0 = pass_on(8, q_out.at[y, a], up)
    t1 = pass_on(9, q_out.at[y, a], down)
    s6.wait_recv()
    s7.wait_recv()
    t2 = pass_on(10, q_out.at[:, b, x], right)
    t3 = pass_on(11, q_out.at[:, b, x], left)
    t0.wait_recv()
    t4 = pass_on(12, q_out.at[ym, 0], up)
    t1.wait_recv()
    t5 = pass_on(13, q_out.at[yp, 1], down)
    t2.wait_recv()
    t6 = pass_on(14, q_out.at[:, 2, xm], right)
    t3.wait_recv()
    t7 = pass_on(15, q_out.at[:, 3, xp], left)
    for cp in (m0, m1, t4, t5, t6, t7):
        cp.wait_recv()
    for cp in (lo, ld):
        cp.wait()
    for cp in waits:
        cp.wait_send()


def gather(queries, lengths, documents):
    hbm = pl.BlockSpec(memory_space=pl.ANY)
    vmem = pl.BlockSpec(memory_space=pltpu.VMEM)
    return pl.pallas_call(
        gather_kernel,
        name="gather_queries",
        out_shape=(
            jax.ShapeDtypeStruct((4, 4, 4, 2, 64, 128), jnp.bfloat16),
            jax.ShapeDtypeStruct((2, 128, CH, 128), jnp.bfloat16),
            jax.ShapeDtypeStruct((2, 8, 128), jnp.int32),
        ),
        in_specs=[vmem, vmem, hbm],
        out_specs=(hbm, hbm, hbm),
        scratch_shapes=[
            pltpu.VMEM((64, 128), jnp.float32),
            pltpu.VMEM((2, 64, 128), jnp.bfloat16),
            pltpu.VMEM((128, 64, 128), jnp.bfloat16),
            pltpu.VMEM((512, 128), jnp.float32),
            pltpu.VMEM((128, CH, 128), jnp.bfloat16),
            pltpu.VMEM((8, 128), jnp.int32),
            pltpu.SMEM((8, 128), jnp.int32),
            pltpu.SemaphoreType.DMA((7,)),
            pltpu.SemaphoreType.DMA((7,)),
            pltpu.SemaphoreType.DMA((16,)),
            pltpu.SemaphoreType.DMA((16,)),
            pltpu.SemaphoreType.DMA((2,)),
            pltpu.SemaphoreType.DMA((2,)),
            pltpu.SemaphoreType.DMA((5,)),
        ],
        compiler_params=pltpu.CompilerParams(collective_id=0, has_side_effects=True, vmem_limit_bytes=60 << 20),
    )(queries, lengths, documents)


def score_kernel(position, *refs):
    pl.run_scoped(
        functools.partial(score_body, position, *refs),
        *([pltpu.ACC(0)((CH, 256), jnp.float32)] * NS + [pltpu.ACC(1)((CH, 256), jnp.float32)] * NS),
    )


def score_body(position, pat_ref, meta_ref, q_hbm, dt_hbm, out_ref,
               qbuf, dt, amax, total, chunks, steps, pairs, sems, *accs):
    acc = (accs[:NS], accs[NS:])
    col = position()
    col = (col, col + 1 - 2 * (col % 2))

    def fetch(side):
        return pltpu.make_async_copy(dt_hbm.at[side], dt.at[pl.ds(side * 128, 128)], sems.at[8 + side])

    def rows_of(k):
        return pltpu.make_async_copy(q_hbm.at[k], qbuf.at[k], sems.at[k])

    def wanted(k):
        return (pat_ref[k, col[0]] > 0) | (pat_ref[k, col[1]] > 0)

    def start(k, _):
        @pl.when(wanted(k))
        def _():
            rows_of(k).start()

        return 0

    lax.fori_loop(0, 8, start, 0)
    fetch(0).start()
    fetch(1).start()
    count = jnp.int32(0)
    for side in range(2):
        def note(k, n, side=side):
            on = pat_ref[k, col[side]] > 0

            @pl.when(on)
            def _():
                pairs[n] = side * 8 + k

            return n + on.astype(jnp.int32)

        count = lax.fori_loop(0, 8, note, count)

        def list_group(g, t, side=side):
            need = (meta_ref[side, 0, g * 8] + 7) // 8

            def put(i, t):
                chunks[side, t] = side * 128 + g * 8 + i
                return t + 1

            return lax.fori_loop(0, need, put, t)

        t = lax.fori_loop(0, 16, list_group, 0)
        for i in range(NS):
            chunks[side, t + i] = chunks[side, t - 1]
        steps[side] = (t + NS - 1) // NS
    units = count * 2
    out_ref[...] = jnp.zeros_like(out_ref)
    total[...] = jnp.zeros_like(total)
    amax[...] = jnp.full_like(amax, -jnp.inf)

    def arrive(k, _):
        @pl.when(wanted(k))
        def _():
            rows_of(k).wait()

        return 0

    lax.fori_loop(0, 8, arrive, 0)
    fetch(0).wait()
    fetch(1).wait()

    def weights(u):
        k = pairs[u // 2] % 8
        for m in range(2):
            j = pl.multiple_of(((u % 2) * 2 + m) * 32, 32)
            w = qbuf[k, :, pl.ds(j, 32), :].reshape(256, 128)
            pltpu.matmul_push_rhs(jnp.concatenate([w, jnp.zeros_like(w)], axis=1), 0, m, transpose=True)

    def push(side, step, s, head=False):
        w = dt[chunks[side, step * NS + s]]
        w = jnp.concatenate([w, jnp.zeros_like(w)], axis=1)
        for m in range(2):
            if head:
                pltpu.matmul_acc_lhs(acc[m][s], w, load_staged_rhs=0)
            else:
                pltpu.matmul_acc_lhs(acc[m][s], w)

    def pop(side, step, s):
        g = (chunks[side, step * NS + s] // 8) % 16
        for m in range(2):
            r = pltpu.matmul_pop(acc[m][s])
            r = jnp.max(r.reshape(8, 8, 256), axis=0)
            amax[g, m] = jnp.maximum(amax[g, m], r)

    def close(slot):
        total[slot] += amax[:, 0] + amax[:, 1]
        amax[...] = jnp.full_like(amax, -jnp.inf)

    @pl.when(count > 0)
    def _():
        weights(0)

        def unit(u, state):
            side0, last0, slot0 = state
            slot = pairs[u // 2]
            side = slot // 8
            for s in range(NS):
                pop(side0, last0, s)
                push(side, 0, s, head=s == 0)
            weights(jnp.minimum(u + 1, units - 1))
            close(slot0)

            def half(m, _):
                for s in range(NS):
                    pop(side, m - 1, s)
                    push(side, m, s)
                return 0

            lax.fori_loop(1, steps[side], half, 0)
            return side, steps[side] - 1, slot

        zero = jnp.int32(0)
        side, last, slot = lax.fori_loop(0, units, unit, (zero, zero, zero + 16))
        for s in range(NS):
            pop(side, last, s)
        close(slot)
        push(0, 0, 0, head=True)
        pltpu.matmul_pop(acc[0][0])
        pltpu.matmul_pop(acc[1][0])

        def finish(i, _):
            slot = pairs[i]
            sums = total[slot].reshape(128, 256)
            for part in range(2):
                turned = sums[:, part * 128:(part + 1) * 128].T.reshape(4, 4, 8, 128)
                folded = (turned[:, 0] + turned[:, 1]) + (turned[:, 2] + turned[:, 3])
                folded = folded[:, 0:4] + folded[:, 4:8]
                out_ref[slot, pl.ds(part * 16, 16)] = folded.reshape(16, 128)
            return 0

        lax.fori_loop(0, count, finish, 0)


def score(position, pattern, meta, rows, dt):
    smem = pl.BlockSpec(memory_space=pltpu.SMEM)
    hbm = pl.BlockSpec(memory_space=pl.ANY)
    return pl.pallas_call(
        functools.partial(score_kernel, position),
        name="score_blocks",
        out_shape=jax.ShapeDtypeStruct((16, 32, 128), jnp.float32),
        in_specs=[smem, smem, hbm, hbm],
        out_specs=pl.BlockSpec(memory_space=pltpu.VMEM),
        scratch_shapes=[
            pltpu.VMEM((8, 8, 128, 128), jnp.bfloat16),
            pltpu.VMEM((256, CH, 128), jnp.bfloat16),
            pltpu.VMEM((16, 2, 8, 256), jnp.float32),
            pltpu.VMEM((17, 16, 8, 256), jnp.float32),
            pltpu.SMEM((2, 128 + NS), jnp.int32),
            pltpu.SMEM((2,), jnp.int32),
            pltpu.SMEM((16,), jnp.int32),
            pltpu.SemaphoreType.DMA((10,)),
        ],
        compiler_params=pltpu.CompilerParams(vmem_limit_bytes=60 << 20),
    )(pattern, meta, rows, dt)


def swap_kernel(part_ref, meta_ref, out_ref, got, s_sem, r_sem):
    idx = lax.axis_index("docs")
    c = idx % 2
    twin = {"docs": idx + 1 - 2 * c, "pb": lax.axis_index("pb")}
    barrier = pltpu.get_barrier_semaphore()
    pl.semaphore_signal(barrier, inc=1, device_id=twin, device_id_type=MESH)
    pl.semaphore_wait(barrier, 1)
    cp = pltpu.make_async_remote_copy(
        src_ref=part_ref.at[pl.ds(8, 8)], dst_ref=got, send_sem=s_sem, recv_sem=r_sem,
        device_id=twin, device_id_type=MESH)
    cp.start()
    rank = jnp.broadcast_to(meta_ref[0, 1:2], (32, 128))

    def place(value, k, core):
        back = jnp.take_along_axis(value, rank, axis=1).reshape(8, 4, 128)
        for h in range(8):
            out_ref[k * 16 + h * 2 + core] = back[h]

    for k in range(8):
        place(part_ref[k], k, c)
    cp.wait_recv()
    for k in range(8):
        place(got[k], k, 1 - c)
    cp.wait_send()


def swap(part, meta):
    vmem = pl.BlockSpec(memory_space=pltpu.VMEM)
    return pl.pallas_call(
        swap_kernel,
        name="swap_scores",
        out_shape=jax.ShapeDtypeStruct((128, 4, 128), jnp.float32),
        in_specs=[vmem, vmem],
        out_specs=vmem,
        scratch_shapes=[
            pltpu.VMEM((8, 32, 128), jnp.float32),
            pltpu.SemaphoreType.DMA,
            pltpu.SemaphoreType.DMA,
        ],
        compiler_params=pltpu.CompilerParams(collective_id=1, has_side_effects=True),
    )(part, meta)


def local(queries, documents, lengths, pattern):
    rows, dt, meta = gather(queries, lengths.reshape(1, 128), documents)
    part = score(lambda: lax.axis_index("docs"), pattern, meta, rows.reshape(8, 8, 128, 128), dt)
    return swap(part, meta)


def solution(mesh):
    return jax.shard_map(
        local,
        mesh=mesh,
        in_specs=(P("docs", "pb", None), P("docs", None, None), P("docs"), P()),
        out_specs=P(None, "pb", "docs"),
        check_vma=False,
    )
```

```python
import functools

import jax
import jax.numpy as jnp
from jax import lax
from jax.experimental import pallas as pl
from jax.experimental.pallas import tpu as pltpu
from jax.sharding import PartitionSpec as P

MESH = pl.DeviceIdType.MESH
CH = 64
NS = 8


def device(y, zl, x, c, h):
    return {"docs": ((y * 4 + zl) * 4 + x) * 2 + c, "pb": h}


def gather_kernel(q_hbm, len_hbm, d_hbm, q_out, dt_out, meta_out,
                  q_ref, len_ref, tmp, prep, docs, wide, dt, meta, meta_s, zs, zr, ss, sr, ts, tr, ls):
    loads = [pltpu.make_async_copy(src, dst, ls.at[5 + n])
             for n, (src, dst) in enumerate(((q_hbm, q_ref), (len_hbm, len_ref), (d_hbm, docs)))]
    for cp in loads:
        cp.start()
    idx = lax.axis_index("docs")
    zh = lax.axis_index("pb")
    c = idx % 2
    x = (idx // 2) % 4
    zl = (idx // 8) % 4
    y = idx // 32
    z = zh * 4 + zl
    xp, xm, yp, ym = (x + 1) % 4, (x + 3) % 4, (y + 1) % 4, (y + 3) % 4
    x2, y2 = (x + 2) % 4, (y + 2) % 4
    right, left = device(y, zl, xp, c, zh), device(y, zl, xm, c, zh)
    up, down = device(yp, zl, x, c, zh), device(ym, zl, x, c, zh)
    twin = device(y, zl, x, 1 - c, zh)
    column = []
    for s in (4, 3, 5, 2, 6, 1, 7):
        zt = (z + s) % 8
        column.append((zt // 4, device(y, zt % 4, x, c, zt // 4)))

    barrier = pltpu.get_barrier_semaphore()
    for d in [d for _, d in column] + [right, left, up, down, twin]:
        pl.semaphore_signal(barrier, inc=1, device_id=d, device_id_type=MESH)

    loads[0].wait()
    for h in range(2):
        for q in range(4):
            tmp[pl.ds(q, 16, stride=4), :] = q_ref[4 * h + q].astype(jnp.float32)
        prep[h] = tmp[...].astype(jnp.bfloat16)

    pl.semaphore_wait(barrier, 12)

    own = q_out.at[y, zl, x, zh]
    waits = []

    def send(src, dst, s_sem, r_sem, d):
        cp = pltpu.make_async_remote_copy(
            src_ref=src, dst_ref=dst, send_sem=s_sem, recv_sem=r_sem, device_id=d, device_id_type=MESH)
        cp.start()
        waits.append(cp)
        return cp

    first = [send(prep.at[ht], own, zs.at[s], zr.at[s], d) for s, (ht, d) in enumerate(column)]
    lc = pltpu.make_async_copy(prep.at[zh], own, ls.at[1])
    lc.start()

    loads[1].wait()
    lanes = jnp.broadcast_to(len_ref[...], (128, 128))
    cols = lanes.T
    r = lax.broadcasted_iota(jnp.int32, (128, 128), 0)
    k = lax.broadcasted_iota(jnp.int32, (128, 128), 1)
    ahead_col = (lanes > cols) | ((lanes == cols) & (k < r))
    ahead_row = (cols > lanes) | ((cols == lanes) & (r < k))
    rank_col = jnp.sum(jnp.where(ahead_col, 1, 0), axis=1, keepdims=True)
    rank_row = jnp.sum(jnp.where(ahead_row, 1, 0), axis=0, keepdims=True)
    here = rank_col == k
    sizes = jnp.sum(jnp.where(here, cols, 0), axis=0, keepdims=True)
    spread = jnp.broadcast_to(sizes, (128, 128))
    need = jnp.where(k % 8 == 0, (spread + 7) // 8, 0)
    steps = jnp.sum(need, axis=1, keepdims=True)[0:1]
    ends = jnp.sum(jnp.where(k <= r, need, 0), axis=1, keepdims=True)
    skip = jnp.where(r % 8 == 0, 8 - (spread.T + 7) // 8, 0)
    place = jnp.minimum(k, steps - 1)
    listed = place[0:1] + jnp.sum(jnp.where(ends <= place, skip, 0), axis=0, keepdims=True)
    meta[0:1] = sizes
    meta[1:2] = rank_row
    meta[2:3] = jnp.sum(jnp.where(here, r, 0), axis=0, keepdims=True)
    meta[3:4] = listed
    meta[4:5] = jnp.broadcast_to(steps, (1, 128))
    meta[5:8] = jnp.zeros((3, 128), jnp.int32)
    lm = pltpu.make_async_copy(meta, meta_s, ls.at[2])
    lm.start()
    lo = pltpu.make_async_copy(meta, meta_out.at[0], ls.at[3])
    lo.start()
    m0 = send(meta, meta_out.at[1], ts.at[0], tr.at[0], twin)
    lm.wait()
    loads[2].wait()

    def arrange(g, _):
        for i in range(8):
            rows = docs[jnp.bitwise_and(meta_s[2, g * 8 + i], 127)].astype(jnp.float32)
            slot = lax.broadcasted_iota(jnp.int32, rows.shape, 0)
            wide[pl.ds(i, 64, stride=8), :] = jnp.where(slot < meta_s[0, g * 8 + i], rows, rows[0:1])
        for i in range(8):
            dt[g * 8 + i] = wide[i * CH:(i + 1) * CH].astype(jnp.bfloat16)
        return 0

    lax.fori_loop(0, 16, arrange, 0)
    ld = pltpu.make_async_copy(dt, dt_out.at[0], ls.at[4])
    ld.start()
    m1 = send(dt, dt_out.at[1], ts.at[1], tr.at[1], twin)

    lc.wait()
    for cp in first:
        cp.wait_recv()

    a = pl.ds(0, 2)
    b = pl.ds(2, 2)
    used = [0]

    def pass_on(ref, d):
        n = used[0]
        used[0] += 1
        return send(ref, ref, ss.at[n], sr.at[n], d)

    def spread_a(xs):
        return pass_on(q_out.at[y, a, xs], up), pass_on(q_out.at[y, a, xs], down)

    def spread_b(ys):
        return pass_on(q_out.at[ys, b, x], right), pass_on(q_out.at[ys, b, x], left)

    def relay_a(xs, pair):
        pair[0].wait_recv()
        f = pass_on(q_out.at[ym, 0, xs], up)
        pair[1].wait_recv()
        return f, pass_on(q_out.at[yp, 1, xs], down)

    def relay_b(ys, pair):
        pair[0].wait_recv()
        f = pass_on(q_out.at[ys, 2, xm], right)
        pair[1].wait_recv()
        return f, pass_on(q_out.at[ys, 3, xp], left)

    s0 = pass_on(q_out.at[y, a, x], right)
    s1 = pass_on(q_out.at[y, a, x], left)
    s2 = pass_on(q_out.at[y, b, x], up)
    s3 = pass_on(q_out.at[y, b, x], down)
    a0 = spread_a(x)
    b0 = spread_b(y)
    s0.wait_recv()
    s4 = pass_on(q_out.at[y, 0, xm], right)
    s1.wait_recv()
    s5 = pass_on(q_out.at[y, 1, xp], left)
    s2.wait_recv()
    s6 = pass_on(q_out.at[ym, 2, x], up)
    s3.wait_recv()
    s7 = pass_on(q_out.at[yp, 3, x], down)
    a1 = spread_a(xm)
    a2 = spread_a(xp)
    b1 = spread_b(ym)
    b2 = spread_b(yp)
    s4.wait_recv()
    s5.wait_recv()
    a3 = spread_a(x2)
    s6.wait_recv()
    s7.wait_recv()
    b3 = spread_b(y2)
    last = []
    for xs, ys, pa, pb in ((x, y, a0, b0), (xm, ym, a1, b1), (xp, yp, a2, b2), (x2, y2, a3, b3)):
        last.extend(relay_a(xs, pa))
        last.extend(relay_b(ys, pb))
    for cp in [m0, m1] + last:
        cp.wait_recv()
    for cp in (lo, ld):
        cp.wait()
    for cp in waits:
        cp.wait_send()


def gather(queries, lengths, documents):
    hbm = pl.BlockSpec(memory_space=pltpu.HBM)
    free = pl.BlockSpec(memory_space=pl.ANY)
    return pl.pallas_call(
        gather_kernel,
        name="gather_queries",
        out_shape=(
            jax.ShapeDtypeStruct((4, 4, 4, 2, 64, 128), jnp.bfloat16),
            jax.ShapeDtypeStruct((2, 128, CH, 128), jnp.bfloat16),
            jax.ShapeDtypeStruct((2, 8, 128), jnp.int32),
        ),
        in_specs=[hbm, hbm, hbm],
        out_specs=(free, free, free),
        scratch_shapes=[
            pltpu.VMEM((8, 16, 128), jnp.bfloat16),
            pltpu.VMEM((1, 128), jnp.int32),
            pltpu.VMEM((64, 128), jnp.float32),
            pltpu.VMEM((2, 64, 128), jnp.bfloat16),
            pltpu.VMEM((128, 64, 128), jnp.bfloat16),
            pltpu.VMEM((512, 128), jnp.float32),
            pltpu.VMEM((128, CH, 128), jnp.bfloat16),
            pltpu.VMEM((8, 128), jnp.int32),
            pltpu.SMEM((8, 128), jnp.int32),
            pltpu.SemaphoreType.DMA((7,)),
            pltpu.SemaphoreType.DMA((7,)),
            pltpu.SemaphoreType.DMA((40,)),
            pltpu.SemaphoreType.DMA((40,)),
            pltpu.SemaphoreType.DMA((2,)),
            pltpu.SemaphoreType.DMA((2,)),
            pltpu.SemaphoreType.DMA((8,)),
        ],
        compiler_params=pltpu.CompilerParams(collective_id=0, has_side_effects=True, vmem_limit_bytes=12 << 20),
    )(*[pltpu.with_memory_space_constraint(v, pltpu.HBM) for v in (queries, lengths, documents)])


def score_kernel(position, *refs):
    pl.run_scoped(
        functools.partial(score_body, position, *refs),
        *([pltpu.ACC(0)((CH, 256), jnp.float32)] * NS + [pltpu.ACC(1)((CH, 256), jnp.float32)] * NS),
    )


def score_body(position, pat_ref, meta_ref, rows, dt, out_ref, amax, total, pairs, *accs):
    acc = (accs[:NS], accs[NS:])
    col = position()
    col = (col, col + 1 - 2 * (col % 2))

    count = jnp.int32(0)
    for side in range(2):
        def note(k, n, side=side):
            on = pat_ref[k, col[side]] > 0

            @pl.when(on)
            def _():
                pairs[n] = side * 8 + k

            return n + on.astype(jnp.int32)

        count = lax.fori_loop(0, 8, note, count)
    steps = [(meta_ref[side, 4, 0] + NS - 1) // NS for side in range(2)]
    out_ref[...] = jnp.zeros_like(out_ref)
    amax[...] = jnp.full_like(amax, -jnp.inf)

    def chunk(side, step, s):
        t = step * NS + s
        return meta_ref[side, 3, t]

    def weights(p):
        k = pairs[p] % 8
        for m in range(2):
            w = [rows[k, :, (2 * half + m) * 32:(2 * half + m + 1) * 32, :].reshape(256, 128) for half in range(2)]
            pltpu.matmul_push_rhs(jnp.concatenate(w, axis=1), 0, m, transpose=True)

    def push(side, step, s, half, head=False):
        w = dt[side, chunk(side, step, s)]
        w = [w, jnp.zeros_like(w)]
        w = jnp.concatenate(w[::-1] if half else w, axis=1)
        for m in range(2):
            if head:
                pltpu.matmul_acc_lhs(acc[m][s], w, load_staged_rhs=0)
            else:
                pltpu.matmul_acc_lhs(acc[m][s], w)

    def pop(side, step, s):
        g = chunk(side, step, s) // 8
        for m in range(2):
            r = pltpu.matmul_pop(acc[m][s])
            r = jnp.max(r.reshape(8, 8, 256), axis=0)
            amax[g, m] = jnp.maximum(amax[g, m], r)

    def close(slot, half):
        value = amax[:, 0] + amax[:, 1]
        total[slot] = total[slot] + value if half else value
        amax[...] = jnp.full_like(amax, -jnp.inf)

    @pl.when(count > 0)
    def _():
        weights(0)

        def one_pair(p, state):
            side0, last0, slot0 = state
            slot = pairs[p]
            side = slot // 8
            n = jnp.where(side == 0, steps[0], steps[1])
            for half in range(2):
                for s in range(NS):
                    if half:
                        pop(side, n - 1, s)
                    else:
                        pop(side0, last0, s)
                    push(side, 0, s, half, head=half == 0 and s == 0)
                if half:
                    close(slot, 0)
                else:
                    weights(jnp.minimum(p + 1, count - 1))
                    close(slot0, 1)

                def further(m, _, half=half):
                    for s in range(NS):
                        pop(side, m - 1, s)
                        push(side, m, s, half)
                    return 0

                lax.fori_loop(1, n, further, 0)
            return side, n - 1, slot

        zero = jnp.int32(0)
        side, last, slot = lax.fori_loop(0, count, one_pair, (zero, zero, zero + 16))
        for s in range(NS):
            pop(side, last, s)
        close(slot, 1)
        push(0, 0, 0, 0, head=True)
        pltpu.matmul_pop(acc[0][0])
        pltpu.matmul_pop(acc[1][0])

        def finish(i, _):
            slot = pairs[i]
            sums = total[slot].reshape(128, 256)
            for part in range(2):
                turned = sums[:, part * 128:(part + 1) * 128].T.reshape(4, 4, 8, 128)
                folded = (turned[:, 0] + turned[:, 1]) + (turned[:, 2] + turned[:, 3])
                folded = folded[:, 0:4] + folded[:, 4:8]
                out_ref[slot, pl.ds(part * 16, 16)] = folded.reshape(16, 128)
            return 0

        lax.fori_loop(0, count, finish, 0)


def score(position, pattern, meta, rows, dt):
    smem = pl.BlockSpec(memory_space=pltpu.SMEM)
    vmem = pl.BlockSpec(memory_space=pltpu.VMEM)
    return pl.pallas_call(
        functools.partial(score_kernel, position),
        name="score_blocks",
        out_shape=jax.ShapeDtypeStruct((16, 32, 128), jnp.float32),
        in_specs=[smem, smem, vmem, vmem],
        out_specs=vmem,
        scratch_shapes=[
            pltpu.VMEM((16, 2, 8, 256), jnp.float32),
            pltpu.VMEM((17, 16, 8, 256), jnp.float32),
            pltpu.SMEM((16,), jnp.int32),
        ],
        compiler_params=pltpu.CompilerParams(vmem_limit_bytes=24 << 20),
    )(pattern, meta, rows, dt)


def swap_kernel(part_ref, meta_ref, out_ref, got, s_sem, r_sem):
    idx = lax.axis_index("docs")
    c = idx % 2
    twin = {"docs": idx + 1 - 2 * c, "pb": lax.axis_index("pb")}
    barrier = pltpu.get_barrier_semaphore()
    pl.semaphore_signal(barrier, inc=1, device_id=twin, device_id_type=MESH)
    pl.semaphore_wait(barrier, 1)
    cp = pltpu.make_async_remote_copy(
        src_ref=part_ref.at[pl.ds(8, 8)], dst_ref=got, send_sem=s_sem, recv_sem=r_sem,
        device_id=twin, device_id_type=MESH)
    cp.start()
    rank = jnp.broadcast_to(meta_ref[0, 1:2], (32, 128))

    def place(value, k, core):
        back = jnp.take_along_axis(value, rank, axis=1).reshape(8, 4, 128)
        for h in range(8):
            out_ref[k * 16 + h * 2 + core] = back[h]

    for k in range(8):
        place(part_ref[k], k, c)
    cp.wait_recv()
    for k in range(8):
        place(got[k], k, 1 - c)
    cp.wait_send()


def swap(part, meta):
    vmem = pl.BlockSpec(memory_space=pltpu.VMEM)
    return pl.pallas_call(
        swap_kernel,
        name="swap_scores",
        out_shape=jax.ShapeDtypeStruct((128, 4, 128), jnp.float32),
        in_specs=[vmem, vmem],
        out_specs=vmem,
        scratch_shapes=[
            pltpu.VMEM((8, 32, 128), jnp.float32),
            pltpu.SemaphoreType.DMA,
            pltpu.SemaphoreType.DMA,
        ],
        compiler_params=pltpu.CompilerParams(collective_id=1, has_side_effects=True, vmem_limit_bytes=4 << 20),
    )(part, meta)


def local(queries, documents, lengths, pattern):
    rows, dt, meta = gather(queries, lengths.reshape(1, 128), documents)
    part = score(lambda: lax.axis_index("docs"), pattern, meta, rows.reshape(8, 8, 128, 128), dt)
    return swap(part, meta)


def solution(mesh):
    return jax.shard_map(
        local,
        mesh=mesh,
        in_specs=(P("docs", "pb", None), P("docs", None, None), P("docs"), P()),
        out_specs=P(None, "pb", "docs"),
        check_vma=False,
    )
```

```python
import functools

import jax
import jax.numpy as jnp
from jax import lax
from jax.experimental import pallas as pl
from jax.experimental.pallas import tpu as pltpu
from jax.sharding import PartitionSpec as P

MESH = pl.DeviceIdType.MESH
CH = 64
NS = 8


def device(y, zl, x, c, h):
    return {"docs": ((y * 4 + zl) * 4 + x) * 2 + c, "pb": h}


def gather_kernel(q_hbm, len_hbm, d_hbm, q_out, dt_out, meta_out,
                  q_ref, len_ref, tmp, prep, docs, wide, dt, meta, meta_s, zs, zr, ss, sr, ts, tr, ls):
    loads = [pltpu.make_async_copy(src, dst, ls.at[5 + n])
             for n, (src, dst) in enumerate(((q_hbm, q_ref), (len_hbm, len_ref), (d_hbm, docs)))]
    for cp in loads:
        cp.start()
    idx = lax.axis_index("docs")
    zh = lax.axis_index("pb")
    c = idx % 2
    x = (idx // 2) % 4
    zl = (idx // 8) % 4
    y = idx // 32
    z = zh * 4 + zl
    xp, xm, yp, ym = (x + 1) % 4, (x + 3) % 4, (y + 1) % 4, (y + 3) % 4
    x2, y2 = (x + 2) % 4, (y + 2) % 4
    right, left = device(y, zl, xp, c, zh), device(y, zl, xm, c, zh)
    up, down = device(yp, zl, x, c, zh), device(ym, zl, x, c, zh)
    twin = device(y, zl, x, 1 - c, zh)
    column = []
    for s in (4, 3, 5, 2, 6, 1, 7):
        zt = (z + s) % 8
        column.append((zt // 4, device(y, zt % 4, x, c, zt // 4)))

    barrier = pltpu.get_barrier_semaphore()
    for d in [d for _, d in column] + [right, left, up, down, twin]:
        pl.semaphore_signal(barrier, inc=1, device_id=d, device_id_type=MESH)

    loads[0].wait()
    for h in range(2):
        for q in range(4):
            tmp[pl.ds(q, 16, stride=4), :] = q_ref[4 * h + q].astype(jnp.float32)
        prep[h] = tmp[...].astype(jnp.bfloat16)

    loads[1].wait()
    lanes = jnp.broadcast_to(len_ref[...], (128, 128))
    cols = lanes.T
    r = lax.broadcasted_iota(jnp.int32, (128, 128), 0)
    k = lax.broadcasted_iota(jnp.int32, (128, 128), 1)
    rs, ks = jnp.maximum(r - 48, 0) // 16, jnp.maximum(k - 48, 0) // 16
    ahead_col = (ks < rs) | ((ks == rs) & ((lanes > cols) | ((lanes == cols) & (k < r))))
    ahead_row = (rs < ks) | ((rs == ks) & ((cols > lanes) | ((cols == lanes) & (r < k))))
    rank_col = jnp.sum(jnp.where(ahead_col, 1, 0), axis=1, keepdims=True)
    here = rank_col == k
    sizes = jnp.sum(jnp.where(here, cols, 0), axis=0, keepdims=True)
    meta[0:1] = sizes
    meta[1:2] = jnp.sum(jnp.where(ahead_row, 1, 0), axis=0, keepdims=True)
    meta[2:3] = jnp.sum(jnp.where(here, r, 0), axis=0, keepdims=True)
    meta[3:4] = (sizes + 7) // 8
    meta[4:8] = jnp.zeros((4, 128), jnp.int32)
    lm = pltpu.make_async_copy(meta, meta_s, ls.at[2])
    lm.start()
    lm.wait()
    share = []

    pl.semaphore_wait(barrier, 12)

    own = q_out.at[y, zl, x, zh]
    waits = []

    def send(src, dst, s_sem, r_sem, d):
        cp = pltpu.make_async_remote_copy(
            src_ref=src, dst_ref=dst, send_sem=s_sem, recv_sem=r_sem, device_id=d, device_id_type=MESH)
        cp.start()
        waits.append(cp)
        return cp

    first = [send(prep.at[ht], own, zs.at[s], zr.at[s], d) for s, (ht, d) in enumerate(column)]
    lc = pltpu.make_async_copy(prep.at[zh], own, ls.at[1])
    lc.start()

    dests = (right, left, up, down)
    lo = pltpu.make_async_copy(meta, meta_out.at[0], ls.at[3])
    lo.start()
    m0 = send(meta, meta_out.at[1], ts.at[0], tr.at[0], twin)
    for n, d in enumerate(dests):
        share.append(send(meta, meta_out.at[2 + 2 * n], ts.at[6 + n], tr.at[6 + n], d))
    loads[2].wait()

    def arrange(g, _):
        for i in range(8):
            rows = docs[jnp.bitwise_and(meta_s[2, g * 8 + i], 127)].astype(jnp.float32)
            slot = lax.broadcasted_iota(jnp.int32, rows.shape, 0)
            wide[pl.ds(i, 64, stride=8), :] = jnp.where(slot < meta_s[0, g * 8 + i], rows, rows[0:1])
        for i in range(8):
            dt[g * 8 + i] = wide[i * CH:(i + 1) * CH].astype(jnp.bfloat16)
        return 0

    lax.fori_loop(8, 16, arrange, 0)
    for n, d in enumerate(dests):
        share.append(send(dt.at[pl.ds(64 + 16 * n, 16)], dt_out.at[pl.ds(128 + 32 * n, 16)],
                          ts.at[2 + n], tr.at[2 + n], d))
    lax.fori_loop(0, 8, arrange, 0)
    ld = pltpu.make_async_copy(dt.at[pl.ds(0, 64)], dt_out.at[pl.ds(0, 64)], ls.at[4])
    ld.start()
    m1 = send(dt.at[pl.ds(0, 64)], dt_out.at[pl.ds(64, 64)], ts.at[1], tr.at[1], twin)

    lc.wait()
    for cp in first:
        cp.wait_recv()

    a = pl.ds(0, 2)
    b = pl.ds(2, 2)
    used = [0]

    def pass_on(ref, d):
        n = used[0]
        used[0] += 1
        return send(ref, ref, ss.at[n], sr.at[n], d)

    def spread_a(xs):
        return pass_on(q_out.at[y, a, xs], up), pass_on(q_out.at[y, a, xs], down)

    def spread_b(ys):
        return pass_on(q_out.at[ys, b, x], right), pass_on(q_out.at[ys, b, x], left)

    def relay_a(xs, pair):
        pair[0].wait_recv()
        f = pass_on(q_out.at[ym, 0, xs], up)
        pair[1].wait_recv()
        return f, pass_on(q_out.at[yp, 1, xs], down)

    def relay_b(ys, pair):
        pair[0].wait_recv()
        f = pass_on(q_out.at[ys, 2, xm], right)
        pair[1].wait_recv()
        return f, pass_on(q_out.at[ys, 3, xp], left)

    s0 = pass_on(q_out.at[y, a, x], right)
    s1 = pass_on(q_out.at[y, a, x], left)
    s2 = pass_on(q_out.at[y, b, x], up)
    s3 = pass_on(q_out.at[y, b, x], down)
    a0 = spread_a(x)
    b0 = spread_b(y)
    s0.wait_recv()
    s4 = pass_on(q_out.at[y, 0, xm], right)
    s1.wait_recv()
    s5 = pass_on(q_out.at[y, 1, xp], left)
    s2.wait_recv()
    s6 = pass_on(q_out.at[ym, 2, x], up)
    s3.wait_recv()
    s7 = pass_on(q_out.at[yp, 3, x], down)
    for n in range(4):
        share[n].wait_recv()
        m2 = meta_out.at[2 + 2 * n]
        share.append(send(m2, meta_out.at[3 + 2 * n], ts.at[14 + n], tr.at[14 + n], twin))
    a1 = spread_a(xm)
    a2 = spread_a(xp)
    b1 = spread_b(ym)
    b2 = spread_b(yp)
    s4.wait_recv()
    s5.wait_recv()
    a3 = spread_a(x2)
    s6.wait_recv()
    s7.wait_recv()
    b3 = spread_b(y2)
    for n in range(4):
        share[4 + n].wait_recv()
        share.append(send(dt_out.at[pl.ds(128 + 32 * n, 16)], dt_out.at[pl.ds(144 + 32 * n, 16)],
                          ts.at[10 + n], tr.at[10 + n], twin))
    last = share[8:]
    for xs, ys, pa, pb in ((x, y, a0, b0), (xm, ym, a1, b1), (xp, yp, a2, b2), (x2, y2, a3, b3)):
        last.extend(relay_a(xs, pa))
        last.extend(relay_b(ys, pb))
    for cp in [m0, m1] + last:
        cp.wait_recv()
    for cp in (lo, ld):
        cp.wait()
    for cp in waits:
        cp.wait_send()


def gather(queries, lengths, documents):
    hbm = pl.BlockSpec(memory_space=pltpu.HBM)
    free = pl.BlockSpec(memory_space=pl.ANY)
    return pl.pallas_call(
        gather_kernel,
        name="gather_queries",
        out_shape=(
            jax.ShapeDtypeStruct((4, 4, 4, 2, 64, 128), jnp.bfloat16),
            jax.ShapeDtypeStruct((256, CH, 128), jnp.bfloat16),
            jax.ShapeDtypeStruct((10, 8, 128), jnp.int32),
        ),
        in_specs=[hbm, hbm, hbm],
        out_specs=(free, free, free),
        scratch_shapes=[
            pltpu.VMEM((8, 16, 128), jnp.bfloat16),
            pltpu.VMEM((1, 128), jnp.int32),
            pltpu.VMEM((64, 128), jnp.float32),
            pltpu.VMEM((2, 64, 128), jnp.bfloat16),
            pltpu.VMEM((128, 64, 128), jnp.bfloat16),
            pltpu.VMEM((512, 128), jnp.float32),
            pltpu.VMEM((128, CH, 128), jnp.bfloat16),
            pltpu.VMEM((8, 128), jnp.int32),
            pltpu.SMEM((8, 128), jnp.int32),
            pltpu.SemaphoreType.DMA((7,)),
            pltpu.SemaphoreType.DMA((7,)),
            pltpu.SemaphoreType.DMA((40,)),
            pltpu.SemaphoreType.DMA((40,)),
            pltpu.SemaphoreType.DMA((18,)),
            pltpu.SemaphoreType.DMA((18,)),
            pltpu.SemaphoreType.DMA((8,)),
        ],
        compiler_params=pltpu.CompilerParams(collective_id=0, has_side_effects=True, vmem_limit_bytes=12 << 20),
    )(*[pltpu.with_memory_space_constraint(v, pltpu.HBM) for v in (queries, lengths, documents)])


def score_kernel(position, *refs):
    pl.run_scoped(
        functools.partial(score_body, position, *refs),
        *([pltpu.ACC(0)((CH, 256), jnp.float32)] * NS + [pltpu.ACC(1)((CH, 256), jnp.float32)] * NS),
    )


def around(idx):
    c, x, zl, y = idx % 2, (idx // 2) % 4, (idx // 8) % 4, idx // 32

    def at(y, x, c):
        return ((y * 4 + zl) * 4 + x) * 2 + c

    xp, xm, yp, ym = (x + 1) % 4, (x + 3) % 4, (y + 1) % 4, (y + 3) % 4
    return c, [[at(v, u, w) for w in (c, 1 - c)] for v, u in ((y, xm), (y, xp), (ym, x), (yp, x))]


def score_body(position, pat_ref, meta_ref, rows, dt, out_ref, amax, total, stage, lists, steps, blocks, *accs):
    acc = (accs[:NS], accs[NS:])
    idx = position()
    c, near = around(idx)
    sides = [(idx, 0, 8, 0, 0), (idx + 1 - 2 * c, 8, 8, 1, 0)]
    for n in range(4):
        for o in range(2):
            sides.append((near[n][o], 16 + 4 * n + 2 * o, 2, 2 + 2 * n + o, 8 + 2 * n))

    def listing(k, n):
        t = jnp.int32(0)
        for col, here, groups, table, there in sides:
            def add(t, here=here, groups=groups, table=table, there=there):
                for g in range(groups):
                    for i in range(8):
                        lists[n, t + i] = (here + g) * 8 + i
                    t = t + meta_ref[table, 3, (there + g) * 8]
                return t

            t = lax.cond(pat_ref[k, col] > 0, add, lambda t: t, t)

        @pl.when(t > 0)
        def _():
            end = lists[n, t - 1]
            for i in range(NS):
                lists[n, t + i] = end
            steps[n] = jnp.right_shift(t + NS - 1, 3)
            blocks[n] = k

        return n + (t > 0).astype(jnp.int32)

    count = lax.fori_loop(0, 8, listing, jnp.int32(0))
    stage[...] = jnp.zeros_like(stage)
    amax[...] = jnp.full_like(amax, -jnp.inf)

    def weights(p):
        k = blocks[p]
        for m in range(2):
            w = [rows[k, :, (2 * half + m) * 32:(2 * half + m + 1) * 32, :].reshape(256, 128) for half in range(2)]
            pltpu.matmul_push_rhs(jnp.concatenate(w, axis=1), 0, m, transpose=True)

    def push(at, half, s, head=False):
        w = dt[at]
        w = [w, jnp.zeros_like(w)]
        w = jnp.concatenate(w[::-1] if half else w, axis=1)
        for m in range(2):
            if head:
                pltpu.matmul_acc_lhs(acc[m][s], w, load_staged_rhs=0)
            else:
                pltpu.matmul_acc_lhs(acc[m][s], w)

    def pop(at, s):
        g = jnp.right_shift(at, 3)
        for m in range(2):
            r = pltpu.matmul_pop(acc[m][s])
            r = jnp.max(r.reshape(8, 8, 256), axis=0)
            amax[g, m] = jnp.maximum(amax[g, m], r)

    def close(p, half):
        value = amax[:, 0] + amax[:, 1]
        total[p] = total[p] + value if half else value
        amax[...] = jnp.full_like(amax, -jnp.inf)

    @pl.when(count > 0)
    def _():
        weights(0)

        def one_block(p, state):
            p0, last0 = state
            n = steps[p]
            for half in range(2):
                before = (p, n - 1) if half else (jnp.maximum(p0, 0), last0)
                olds = [lists[before[0], before[1] * NS + s] for s in range(NS)]
                news = [lists[p, s] for s in range(NS)]
                for s in range(NS):
                    pop(olds[s], s)
                    push(news[s], half, s, head=half == 0 and s == 0)
                if half:
                    close(p, 0)
                else:
                    weights(jnp.minimum(p + 1, count - 1))
                    close(jnp.where(p0 < 0, 8, p0), 1)

                def further(m, _, half=half):
                    olds = [lists[p, (m - 1) * NS + s] for s in range(NS)]
                    news = [lists[p, m * NS + s] for s in range(NS)]
                    for s in range(NS):
                        pop(olds[s], s)
                        push(news[s], half, s)
                    return 0

                lax.fori_loop(1, n, further, 0)
            return p, n - 1

        zero = jnp.int32(0)
        p, last = lax.fori_loop(0, count, one_block, (zero - 1, zero))
        for s in range(NS):
            pop(lists[p, last * NS + s], s)
        close(p, 1)
        push(0, 0, 0, head=True)
        pltpu.matmul_pop(acc[0][0])
        pltpu.matmul_pop(acc[1][0])

        lane = lax.broadcasted_iota(jnp.int32, (32, 128), 1)

        def finish(p, _):
            k = blocks[p]
            flags = [pat_ref[k, side[0]] for side in sides]
            for part in range(2):
                on = jnp.zeros((32, 128), jnp.int32)
                for flag, (_, here, groups, _, _) in zip(flags, sides):
                    if here // 16 == part:
                        low = (here % 16) * 8
                        on = jnp.where((lane >= low) & (lane < low + groups * 8), flag, on)
                sums = total[p, part * 16:(part + 1) * 16].reshape(128, 256)
                for h in range(2):
                    turned = sums[:, h * 128:(h + 1) * 128].T.reshape(4, 4, 8, 128)
                    folded = (turned[:, 0] + turned[:, 1]) + (turned[:, 2] + turned[:, 3])
                    folded = (folded[:, 0:4] + folded[:, 4:8]).reshape(16, 128)
                    stage[k // 4, pl.ds(pl.multiple_of((k % 4) * 32 + h * 16, 16), 16), part * 128:(part + 1) * 128] = (
                        jnp.where(on[:16] > 0, folded, 0.0))
            return 0

        lax.fori_loop(0, count, finish, 0)

    for side in range(2):
        for part in range(2):
            out_ref[side, part * 128:(part + 1) * 128] = stage[side, :, part * 128:(part + 1) * 128].T


def score(position, pattern, meta, rows, dt):
    smem = pl.BlockSpec(memory_space=pltpu.SMEM)
    vmem = pl.BlockSpec(memory_space=pltpu.VMEM)
    return pl.pallas_call(
        functools.partial(score_kernel, position),
        name="score_blocks",
        out_shape=jax.ShapeDtypeStruct((2, 256, 128), jnp.float32),
        in_specs=[smem, smem, vmem, vmem],
        out_specs=vmem,
        scratch_shapes=[
            pltpu.VMEM((32, 2, 8, 256), jnp.float32),
            pltpu.VMEM((9, 32, 8, 256), jnp.float32),
            pltpu.VMEM((2, 128, 256), jnp.float32),
            pltpu.SMEM((8, 256 + NS), jnp.int32),
            pltpu.SMEM((8,), jnp.int32),
            pltpu.SMEM((8,), jnp.int32),
        ],
        compiler_params=pltpu.CompilerParams(vmem_limit_bytes=24 << 20),
    )(pattern, meta, rows, dt)


def swap_kernel(part_ref, meta_ref, out_ref, got, s_sem, r_sem):
    idx = lax.axis_index("docs")
    zh = lax.axis_index("pb")
    c, near = around(idx)
    twin = {"docs": idx + 1 - 2 * c, "pb": zh}
    partners = [{"docs": near[n][o], "pb": zh} for n in range(4) for o in range(2)]
    barrier = pltpu.get_barrier_semaphore()
    for d in partners + [twin]:
        pl.semaphore_signal(barrier, inc=1, device_id=d, device_id_type=MESH)
    pl.semaphore_wait(barrier, 9)
    copies = []
    for n in range(4):
        for o in range(2):
            q = 2 * n + o
            copies.append(pltpu.make_async_remote_copy(
                src_ref=part_ref.at[:, pl.ds(128 + 16 * q, 16)], dst_ref=got.at[c, :, pl.ds(64 + 16 * n, 16)],
                send_sem=s_sem.at[q], recv_sem=r_sem.at[q], device_id=partners[q], device_id_type=MESH))
    copies.append(pltpu.make_async_remote_copy(
        src_ref=part_ref.at[:, pl.ds(64, 64)], dst_ref=got.at[c, :, pl.ds(0, 64)],
        send_sem=s_sem.at[8], recv_sem=r_sem.at[8], device_id=twin, device_id_type=MESH))
    for cp in copies:
        cp.start()
    got[c, :, 0:64] = part_ref[:, 0:64]
    rank = jnp.broadcast_to(meta_ref[0, 1:2], (128, 128))
    for cp in copies:
        cp.wait_recv()
    for core in range(2):
        for half in range(2):
            back = jnp.take_along_axis(got[core, half].T, rank, axis=1).reshape(4, 8, 4, 128)
            for k in range(4):
                for h in range(8):
                    out_ref[(half * 4 + k) * 16 + h * 2 + core] = back[k, h]
    for cp in copies:
        cp.wait_send()


def swap(part, meta):
    vmem = pl.BlockSpec(memory_space=pltpu.VMEM)
    return pl.pallas_call(
        swap_kernel,
        name="swap_scores",
        out_shape=jax.ShapeDtypeStruct((128, 4, 128), jnp.float32),
        in_specs=[vmem, vmem],
        out_specs=vmem,
        scratch_shapes=[
            pltpu.VMEM((2, 2, 128, 128), jnp.float32),
            pltpu.SemaphoreType.DMA((9,)),
            pltpu.SemaphoreType.DMA((9,)),
        ],
        compiler_params=pltpu.CompilerParams(collective_id=1, has_side_effects=True, vmem_limit_bytes=4 << 20),
    )(part, meta)


def local(queries, documents, lengths, pattern):
    rows, dt, meta = gather(queries, lengths.reshape(1, 128), documents)
    part = score(lambda: lax.axis_index("docs"), pattern, meta, rows.reshape(8, 8, 128, 128), dt)
    return swap(part, meta)


def solution(mesh):
    return jax.shard_map(
        local,
        mesh=mesh,
        in_specs=(P("docs", "pb", None), P("docs", None, None), P("docs"), P()),
        out_specs=P(None, "pb", "docs"),
        check_vma=False,
    )
```

```python
import functools

import jax
import jax.numpy as jnp
from jax import lax
from jax.experimental import pallas as pl
from jax.experimental.pallas import tpu as pltpu
from jax.sharding import PartitionSpec as P

MESH = pl.DeviceIdType.MESH
CH = 64
NS = 12
RUN = NS // 2


def device(y, zl, x, c, h):
    return {"docs": ((y * 4 + zl) * 4 + x) * 2 + c, "pb": h}


def gather_kernel(q_hbm, len_hbm, d_hbm, q_out, dt_out, meta_out,
                  q_ref, len_ref, tmp, prep, docs, wide, dt, meta, meta_s, zs, zr, ss, sr, ts, tr, ls):
    loads = [pltpu.make_async_copy(src, dst, ls.at[5 + n])
             for n, (src, dst) in enumerate(((q_hbm, q_ref), (len_hbm, len_ref), (d_hbm, docs)))]
    for cp in loads:
        cp.start()
    idx = lax.axis_index("docs")
    zh = lax.axis_index("pb")
    c = idx % 2
    x = (idx // 2) % 4
    zl = (idx // 8) % 4
    y = idx // 32
    z = zh * 4 + zl
    xp, xm, yp, ym = (x + 1) % 4, (x + 3) % 4, (y + 1) % 4, (y + 3) % 4
    x2, y2 = (x + 2) % 4, (y + 2) % 4
    right, left = device(y, zl, xp, c, zh), device(y, zl, xm, c, zh)
    up, down = device(yp, zl, x, c, zh), device(ym, zl, x, c, zh)
    twin = device(y, zl, x, 1 - c, zh)
    column = []
    for s in (4, 3, 5, 2, 6, 1, 7):
        zt = (z + s) % 8
        column.append((zt // 4, device(y, zt % 4, x, c, zt // 4)))

    barrier = pltpu.get_barrier_semaphore()
    for d in [d for _, d in column] + [right, left, up, down, twin]:
        pl.semaphore_signal(barrier, inc=1, device_id=d, device_id_type=MESH)

    loads[0].wait()
    for h in range(2):
        for q in range(4):
            tmp[pl.ds(q, 16, stride=4), :] = q_ref[4 * h + q].astype(jnp.float32)
        prep[h] = tmp[...].astype(jnp.bfloat16)

    loads[1].wait()
    lanes = jnp.broadcast_to(len_ref[...], (128, 128))
    cols = lanes.T
    r = lax.broadcasted_iota(jnp.int32, (128, 128), 0)
    k = lax.broadcasted_iota(jnp.int32, (128, 128), 1)
    rs, ks = jnp.maximum(r - 48, 0) // 16, jnp.maximum(k - 48, 0) // 16
    ahead_col = (ks < rs) | ((ks == rs) & ((lanes > cols) | ((lanes == cols) & (k < r))))
    ahead_row = (rs < ks) | ((rs == ks) & ((cols > lanes) | ((cols == lanes) & (r < k))))
    rank_col = jnp.sum(jnp.where(ahead_col, 1, 0), axis=1, keepdims=True)
    here = rank_col == k
    sizes = jnp.sum(jnp.where(here, cols, 0), axis=0, keepdims=True)
    meta[0:1] = sizes
    meta[1:2] = jnp.sum(jnp.where(ahead_row, 1, 0), axis=0, keepdims=True)
    meta[2:3] = jnp.sum(jnp.where(here, r, 0), axis=0, keepdims=True)
    meta[3:4] = (sizes + 7) // 8
    meta[4:8] = jnp.zeros((4, 128), jnp.int32)
    lm = pltpu.make_async_copy(meta, meta_s, ls.at[2])
    lm.start()
    lm.wait()
    share = []
    loads[2].wait()

    def arrange(g, _):
        for i in range(8):
            rows = docs[jnp.bitwise_and(meta_s[2, g * 8 + i], 127)].astype(jnp.float32)
            slot = lax.broadcasted_iota(jnp.int32, rows.shape, 0)
            wide[pl.ds(i, 64, stride=8), :] = jnp.where(slot < meta_s[0, g * 8 + i], rows, rows[0:1])
        for i in range(8):
            dt[g * 8 + i] = wide[i * CH:(i + 1) * CH].astype(jnp.bfloat16)
        return 0

    lax.fori_loop(8, 16, arrange, 0)
    pl.semaphore_wait(barrier, 12)

    own = q_out.at[y, zl, x, zh]
    waits = []

    def send(src, dst, s_sem, r_sem, d):
        cp = pltpu.make_async_remote_copy(
            src_ref=src, dst_ref=dst, send_sem=s_sem, recv_sem=r_sem, device_id=d, device_id_type=MESH)
        cp.start()
        waits.append(cp)
        return cp

    first = [send(prep.at[ht], own, zs.at[s], zr.at[s], d) for s, (ht, d) in enumerate(column)]
    lc = pltpu.make_async_copy(prep.at[zh], own, ls.at[1])
    lc.start()

    dests = (right, left, up, down)
    lo = pltpu.make_async_copy(meta, meta_out.at[0], ls.at[3])
    lo.start()
    m0 = send(meta, meta_out.at[1], ts.at[0], tr.at[0], twin)
    for n, d in enumerate(dests):
        share.append(send(meta, meta_out.at[2 + 2 * n], ts.at[6 + n], tr.at[6 + n], d))
    for n, d in enumerate(dests):
        share.append(send(dt.at[pl.ds(64 + 16 * n, 16)], dt_out.at[pl.ds(128 + 32 * n, 16)],
                          ts.at[2 + n], tr.at[2 + n], d))
    lax.fori_loop(0, 8, arrange, 0)
    ld = pltpu.make_async_copy(dt.at[pl.ds(0, 64)], dt_out.at[pl.ds(0, 64)], ls.at[4])
    ld.start()
    m1 = send(dt.at[pl.ds(0, 64)], dt_out.at[pl.ds(64, 64)], ts.at[1], tr.at[1], twin)

    lc.wait()
    for cp in first:
        cp.wait_recv()

    a = pl.ds(0, 2)
    b = pl.ds(2, 2)
    used = [0]

    def pass_on(ref, d):
        n = used[0]
        used[0] += 1
        return send(ref, ref, ss.at[n], sr.at[n], d)

    def spread_a(xs):
        return pass_on(q_out.at[y, a, xs], up), pass_on(q_out.at[y, a, xs], down)

    def spread_b(ys):
        return pass_on(q_out.at[ys, b, x], right), pass_on(q_out.at[ys, b, x], left)

    def relay_a(xs, pair):
        pair[0].wait_recv()
        f = pass_on(q_out.at[ym, 0, xs], up)
        pair[1].wait_recv()
        return f, pass_on(q_out.at[yp, 1, xs], down)

    def relay_b(ys, pair):
        pair[0].wait_recv()
        f = pass_on(q_out.at[ys, 2, xm], right)
        pair[1].wait_recv()
        return f, pass_on(q_out.at[ys, 3, xp], left)

    s0 = pass_on(q_out.at[y, a, x], right)
    s1 = pass_on(q_out.at[y, a, x], left)
    s2 = pass_on(q_out.at[y, b, x], up)
    s3 = pass_on(q_out.at[y, b, x], down)
    a0 = spread_a(x)
    b0 = spread_b(y)
    s0.wait_recv()
    s4 = pass_on(q_out.at[y, 0, xm], right)
    s1.wait_recv()
    s5 = pass_on(q_out.at[y, 1, xp], left)
    s2.wait_recv()
    s6 = pass_on(q_out.at[ym, 2, x], up)
    s3.wait_recv()
    s7 = pass_on(q_out.at[yp, 3, x], down)
    for n in range(4):
        share[n].wait_recv()
        m2 = meta_out.at[2 + 2 * n]
        share.append(send(m2, meta_out.at[3 + 2 * n], ts.at[14 + n], tr.at[14 + n], twin))
    a1 = spread_a(xm)
    a2 = spread_a(xp)
    b1 = spread_b(ym)
    b2 = spread_b(yp)
    s4.wait_recv()
    s5.wait_recv()
    a3 = spread_a(x2)
    s6.wait_recv()
    s7.wait_recv()
    b3 = spread_b(y2)
    for n in range(4):
        share[4 + n].wait_recv()
        share.append(send(dt_out.at[pl.ds(128 + 32 * n, 16)], dt_out.at[pl.ds(144 + 32 * n, 16)],
                          ts.at[10 + n], tr.at[10 + n], twin))
    last = share[8:]
    for xs, ys, pa, pb in ((x, y, a0, b0), (xm, ym, a1, b1), (xp, yp, a2, b2), (x2, y2, a3, b3)):
        last.extend(relay_a(xs, pa))
        last.extend(relay_b(ys, pb))
    for cp in [m0, m1] + last:
        cp.wait_recv()
    for cp in (lo, ld):
        cp.wait()
    for cp in waits:
        cp.wait_send()


def gather(queries, lengths, documents):
    hbm = pl.BlockSpec(memory_space=pltpu.HBM)
    free = pl.BlockSpec(memory_space=pl.ANY)
    return pl.pallas_call(
        gather_kernel,
        name="gather_queries",
        out_shape=(
            jax.ShapeDtypeStruct((4, 4, 4, 2, 64, 128), jnp.bfloat16),
            jax.ShapeDtypeStruct((256, CH, 128), jnp.bfloat16),
            jax.ShapeDtypeStruct((10, 8, 128), jnp.int32),
        ),
        in_specs=[hbm, hbm, hbm],
        out_specs=(free, free, free),
        scratch_shapes=[
            pltpu.VMEM((8, 16, 128), jnp.bfloat16),
            pltpu.VMEM((1, 128), jnp.int32),
            pltpu.VMEM((64, 128), jnp.float32),
            pltpu.VMEM((2, 64, 128), jnp.bfloat16),
            pltpu.VMEM((128, 64, 128), jnp.bfloat16),
            pltpu.VMEM((512, 128), jnp.float32),
            pltpu.VMEM((128, CH, 128), jnp.bfloat16),
            pltpu.VMEM((8, 128), jnp.int32),
            pltpu.SMEM((8, 128), jnp.int32),
            pltpu.SemaphoreType.DMA((7,)),
            pltpu.SemaphoreType.DMA((7,)),
            pltpu.SemaphoreType.DMA((40,)),
            pltpu.SemaphoreType.DMA((40,)),
            pltpu.SemaphoreType.DMA((18,)),
            pltpu.SemaphoreType.DMA((18,)),
            pltpu.SemaphoreType.DMA((8,)),
        ],
        compiler_params=pltpu.CompilerParams(collective_id=0, has_side_effects=True, vmem_limit_bytes=12 << 20),
    )(*[pltpu.with_memory_space_constraint(v, pltpu.HBM) for v in (queries, lengths, documents)])


def score_kernel(position, *refs):
    pl.run_scoped(
        functools.partial(score_body, position, *refs),
        *([pltpu.ACC(0)((CH, 256), jnp.float32)] * NS + [pltpu.ACC(1)((CH, 256), jnp.float32)] * NS),
    )


def around(idx):
    c, x, zl, y = idx % 2, (idx // 2) % 4, (idx // 8) % 4, idx // 32

    def at(y, x, c):
        return ((y * 4 + zl) * 4 + x) * 2 + c

    xp, xm, yp, ym = (x + 1) % 4, (x + 3) % 4, (y + 1) % 4, (y + 3) % 4
    return c, [[at(v, u, w) for w in (c, 1 - c)] for v, u in ((y, xm), (y, xp), (ym, x), (yp, x))]


def score_body(position, pat_ref, meta_ref, rows, dt, out_ref, amax, total, stage, lists, steps, blocks, *accs):
    acc = (accs[:NS], accs[NS:])
    idx = position()
    c, near = around(idx)
    sides = [(idx, 0, 8, 0, 0), (idx + 1 - 2 * c, 8, 8, 1, 0)]
    for n in range(4):
        for o in range(2):
            sides.append((near[n][o], 16 + 4 * n + 2 * o, 2, 2 + 2 * n + o, 8 + 2 * n))

    def listing(k, n):
        t = jnp.int32(0)
        for col, here, groups, table, there in sides:
            def add(t, here=here, groups=groups, table=table, there=there):
                for g in range(groups):
                    for i in range(8):
                        lists[n, t + i] = (here + g) * 8 + i
                    t = t + meta_ref[table, 3, (there + g) * 8]
                return t

            t = lax.cond(pat_ref[k, col] > 0, add, lambda t: t, t)

        @pl.when(t > 0)
        def _():
            end = lists[n, t - 1]
            for i in range(RUN):
                lists[n, t + i] = end
            steps[n] = (t + RUN - 1) // RUN
            blocks[n] = k

        return n + (t > 0).astype(jnp.int32)

    count = lax.fori_loop(0, 8, listing, jnp.int32(0))
    stage[...] = jnp.zeros_like(stage)

    def weights(p):
        k = blocks[p]
        for m in range(2):
            w = []
            for half in range(2):
                low = (2 * half + m) * 32
                w.append(jnp.concatenate([rows[k, :, low + 16 * t:low + 16 * t + 16, :].reshape(128, 128) for t in range(2)], axis=0))
            pltpu.matmul_push_rhs(jnp.concatenate(w, axis=1), 0, m, transpose=True)

    def push(at, s, head=False):
        w = dt[at]
        for half in range(2):
            v = [w, jnp.zeros_like(w)]
            v = jnp.concatenate(v[::-1] if half else v, axis=1)
            for m in range(2):
                if head and half == 0:
                    pltpu.matmul_acc_lhs(acc[m][2 * s], v, load_staged_rhs=0)
                else:
                    pltpu.matmul_acc_lhs(acc[m][2 * s + half], v)

    def pop(at, s, tops):
        g = jnp.right_shift(at, 3)
        roof = jnp.where(jnp.bitwise_and(at, 7) == 0, -jnp.inf, jnp.inf).astype(jnp.float32)
        after = []
        for half in range(2):
            for m in range(2):
                r = pltpu.matmul_pop(acc[m][2 * s + half])
                r = jnp.max(r.reshape(8, 8, 256), axis=0)
                r = jnp.maximum(jnp.minimum(tops[2 * half + m], roof), r)
                amax[g, 2 * half + m] = r
                after.append(r)
        return after

    def close(p):
        value = (amax[:, 0] + amax[:, 1]) + (amax[:, 2] + amax[:, 3])
        total[p] = value[:, :, :128] + value[:, :, 128:]

    @pl.when(count > 0)
    def _():
        weights(0)

        def one_block(p, state):
            p0, last0, tops = state
            n = steps[p]
            olds = [lists[jnp.maximum(p0, 0), last0 * RUN + s] for s in range(RUN)]
            news = [lists[p, s] for s in range(RUN)]
            for s in range(RUN):
                tops = pop(olds[s], s, tops)
                push(news[s], s, head=s == 0)
            weights(jnp.minimum(p + 1, count - 1))
            close(jnp.where(p0 < 0, 8, p0))

            def further(m, tops):
                olds = [lists[p, (m - 1) * RUN + s] for s in range(RUN)]
                news = [lists[p, m * RUN + s] for s in range(RUN)]
                for s in range(RUN):
                    tops = pop(olds[s], s, tops)
                    push(news[s], s)
                return tops

            return p, n - 1, lax.fori_loop(1, n, further, tops)

        zero = jnp.int32(0)
        start = [jnp.full((8, 256), -jnp.inf, jnp.float32)] * 4
        p, last, tops = lax.fori_loop(0, count, one_block, (zero - 1, zero, start))
        for s in range(RUN):
            tops = pop(lists[p, last * RUN + s], s, tops)
        close(p)
        push(0, 0, head=True)
        for half in range(2):
            for m in range(2):
                pltpu.matmul_pop(acc[m][half])

        lane = lax.broadcasted_iota(jnp.int32, (32, 128), 1)

        def finish(p, _):
            k = blocks[p]
            flags = [pat_ref[k, side[0]] for side in sides]
            for part in range(2):
                on = jnp.zeros((32, 128), jnp.int32)
                for flag, (_, here, groups, _, _) in zip(flags, sides):
                    if here // 16 == part:
                        low = (here % 16) * 8
                        on = jnp.where((lane >= low) & (lane < low + groups * 8), flag, on)
                turned = total[p, part * 16:(part + 1) * 16].reshape(128, 128).T.reshape(8, 2, 8, 128)
                folded = turned[:, 0] + turned[:, 1]
                folded = (folded[:, 0:4] + folded[:, 4:8]).reshape(32, 128)
                stage[k // 4, pl.ds(pl.multiple_of((k % 4) * 32, 32), 32), part * 128:(part + 1) * 128] = (
                    jnp.where(on > 0, folded, 0.0))
            return 0

        lax.fori_loop(0, count, finish, 0)

    for side in range(2):
        for part in range(2):
            out_ref[side, part * 128:(part + 1) * 128] = stage[side, :, part * 128:(part + 1) * 128].T


def score(position, pattern, meta, rows, dt):
    smem = pl.BlockSpec(memory_space=pltpu.SMEM)
    vmem = pl.BlockSpec(memory_space=pltpu.VMEM)
    return pl.pallas_call(
        functools.partial(score_kernel, position),
        name="score_blocks",
        out_shape=jax.ShapeDtypeStruct((2, 256, 128), jnp.float32),
        in_specs=[smem, smem, vmem, vmem],
        out_specs=vmem,
        scratch_shapes=[
            pltpu.VMEM((32, 4, 8, 256), jnp.float32),
            pltpu.VMEM((9, 32, 8, 128), jnp.float32),
            pltpu.VMEM((2, 128, 256), jnp.float32),
            pltpu.SMEM((8, 256 + NS), jnp.int32),
            pltpu.SMEM((8,), jnp.int32),
            pltpu.SMEM((8,), jnp.int32),
        ],
        compiler_params=pltpu.CompilerParams(vmem_limit_bytes=24 << 20),
    )(pattern, meta, rows, dt)


def swap_kernel(part_ref, meta_ref, out_ref, got, s_sem, r_sem):
    idx = lax.axis_index("docs")
    zh = lax.axis_index("pb")
    c, near = around(idx)
    twin = {"docs": idx + 1 - 2 * c, "pb": zh}
    partners = [{"docs": near[n][o], "pb": zh} for n in range(4) for o in range(2)]
    barrier = pltpu.get_barrier_semaphore()
    for d in partners + [twin]:
        pl.semaphore_signal(barrier, inc=1, device_id=d, device_id_type=MESH)
    pl.semaphore_wait(barrier, 9)
    copies = []
    for n in range(4):
        for o in range(2):
            q = 2 * n + o
            copies.append(pltpu.make_async_remote_copy(
                src_ref=part_ref.at[:, pl.ds(128 + 16 * q, 16)], dst_ref=got.at[c, :, pl.ds(64 + 16 * n, 16)],
                send_sem=s_sem.at[q], recv_sem=r_sem.at[q], device_id=partners[q], device_id_type=MESH))
    copies.append(pltpu.make_async_remote_copy(
        src_ref=part_ref.at[:, pl.ds(64, 64)], dst_ref=got.at[c, :, pl.ds(0, 64)],
        send_sem=s_sem.at[8], recv_sem=r_sem.at[8], device_id=twin, device_id_type=MESH))
    for cp in copies:
        cp.start()
    got[c, :, 0:64] = part_ref[:, 0:64]
    rank = jnp.broadcast_to(meta_ref[0, 1:2], (128, 128))
    for cp in copies:
        cp.wait_recv()
    for core in range(2):
        for half in range(2):
            back = jnp.take_along_axis(got[core, half].T, rank, axis=1).reshape(4, 8, 4, 128)
            for k in range(4):
                for h in range(8):
                    out_ref[(half * 4 + k) * 16 + h * 2 + core] = back[k, h]
    for cp in copies:
        cp.wait_send()


def swap(part, meta):
    vmem = pl.BlockSpec(memory_space=pltpu.VMEM)
    return pl.pallas_call(
        swap_kernel,
        name="swap_scores",
        out_shape=jax.ShapeDtypeStruct((128, 4, 128), jnp.float32),
        in_specs=[vmem, vmem],
        out_specs=vmem,
        scratch_shapes=[
            pltpu.VMEM((2, 2, 128, 128), jnp.float32),
            pltpu.SemaphoreType.DMA((9,)),
            pltpu.SemaphoreType.DMA((9,)),
        ],
        compiler_params=pltpu.CompilerParams(collective_id=1, has_side_effects=True, vmem_limit_bytes=4 << 20),
    )(part, meta)


def local(queries, documents, lengths, pattern):
    rows, dt, meta = gather(queries, lengths.reshape(1, 128), documents)
    part = score(lambda: lax.axis_index("docs"), pattern, meta, rows.reshape(8, 8, 128, 128), dt)
    return swap(part, meta)


def solution(mesh):
    return jax.shard_map(
        local,
        mesh=mesh,
        in_specs=(P("docs", "pb", None), P("docs", None, None), P("docs"), P()),
        out_specs=P(None, "pb", "docs"),
        check_vma=False,
    )
```

```python
import functools

import jax
import jax.numpy as jnp
from jax import lax
from jax.experimental import pallas as pl
from jax.experimental.pallas import tpu as pltpu
from jax.sharding import PartitionSpec as P

MESH = pl.DeviceIdType.MESH
CH = 64
NS = 12
RUN = NS // 2


def device(y, zl, x, c, h):
    return {"docs": ((y * 4 + zl) * 4 + x) * 2 + c, "pb": h}


SHARES = (0, 2, 4, 6, 9, 11, 13, 15, 1, 14, 3, 12, 5, 10, 7, 8)


def placed(rank):
    group = rank // 8
    slot = jnp.zeros_like(rank)
    for n, g in enumerate(SHARES):
        slot = jnp.where(group == g, n, slot)
    return slot * 8 + rank % 8


def gather_kernel(q_hbm, len_hbm, d_hbm, q_out, dt_out, meta_out,
                  q_ref, len_ref, tmp, prep, docs, wide, dt, meta, meta_s, zs, zr, ss, sr, ts, tr, ls):
    loads = [pltpu.make_async_copy(src, dst, ls.at[5 + n])
             for n, (src, dst) in enumerate(((q_hbm, q_ref), (len_hbm, len_ref), (d_hbm, docs)))]
    for cp in loads:
        cp.start()
    idx = lax.axis_index("docs")
    zh = lax.axis_index("pb")
    c = idx % 2
    x = (idx // 2) % 4
    zl = (idx // 8) % 4
    y = idx // 32
    z = zh * 4 + zl
    xp, xm, yp, ym = (x + 1) % 4, (x + 3) % 4, (y + 1) % 4, (y + 3) % 4
    x2, y2 = (x + 2) % 4, (y + 2) % 4
    right, left = device(y, zl, xp, c, zh), device(y, zl, xm, c, zh)
    up, down = device(yp, zl, x, c, zh), device(ym, zl, x, c, zh)
    twin = device(y, zl, x, 1 - c, zh)
    column = []
    for s in (4, 3, 5, 2, 6, 1, 7):
        zt = (z + s) % 8
        column.append((zt // 4, device(y, zt % 4, x, c, zt // 4)))

    barrier = pltpu.get_barrier_semaphore()
    for d in [d for _, d in column] + [right, left, up, down, twin]:
        pl.semaphore_signal(barrier, inc=1, device_id=d, device_id_type=MESH)

    loads[0].wait()
    for h in range(2):
        for q in range(4):
            tmp[pl.ds(q, 16, stride=4), :] = q_ref[4 * h + q].astype(jnp.float32)
        prep[h] = tmp[...].astype(jnp.bfloat16)

    loads[1].wait()
    lanes = jnp.broadcast_to(len_ref[...], (128, 128))
    cols = lanes.T
    r = lax.broadcasted_iota(jnp.int32, (128, 128), 0)
    k = lax.broadcasted_iota(jnp.int32, (128, 128), 1)
    ahead_col = (lanes > cols) | ((lanes == cols) & (k < r))
    ahead_row = (cols > lanes) | ((cols == lanes) & (r < k))
    rank_col = placed(jnp.sum(jnp.where(ahead_col, 1, 0), axis=1, keepdims=True))
    rank_row = placed(jnp.sum(jnp.where(ahead_row, 1, 0), axis=0, keepdims=True))
    here = rank_col == k
    sizes = jnp.sum(jnp.where(here, cols, 0), axis=0, keepdims=True)
    meta[0:1] = sizes
    meta[1:2] = rank_row
    meta[2:3] = jnp.sum(jnp.where(here, r, 0), axis=0, keepdims=True)
    meta[3:4] = (sizes + 7) // 8
    meta[4:8] = jnp.zeros((4, 128), jnp.int32)
    lm = pltpu.make_async_copy(meta, meta_s, ls.at[2])
    lm.start()
    lm.wait()
    share = []
    loads[2].wait()

    def arrange(g, _):
        for i in range(8):
            rows = docs[jnp.bitwise_and(meta_s[2, g * 8 + i], 127)].astype(jnp.float32)
            slot = lax.broadcasted_iota(jnp.int32, rows.shape, 0)
            wide[pl.ds(i, 64, stride=8), :] = jnp.where(slot < meta_s[0, g * 8 + i], rows, rows[0:1])
        for i in range(8):
            dt[g * 8 + i] = wide[i * CH:(i + 1) * CH].astype(jnp.bfloat16)
        return 0

    lax.fori_loop(8, 16, arrange, 0)
    pl.semaphore_wait(barrier, 12)

    own = q_out.at[y, zl, x, zh]
    waits = []

    def send(src, dst, s_sem, r_sem, d):
        cp = pltpu.make_async_remote_copy(
            src_ref=src, dst_ref=dst, send_sem=s_sem, recv_sem=r_sem, device_id=d, device_id_type=MESH)
        cp.start()
        waits.append(cp)
        return cp

    first = [send(prep.at[ht], own, zs.at[s], zr.at[s], d) for s, (ht, d) in enumerate(column)]
    lc = pltpu.make_async_copy(prep.at[zh], own, ls.at[1])
    lc.start()

    dests = (right, left, up, down)
    lo = pltpu.make_async_copy(meta, meta_out.at[0], ls.at[3])
    lo.start()
    m0 = send(meta, meta_out.at[1], ts.at[0], tr.at[0], twin)
    for n, d in enumerate(dests):
        share.append(send(meta, meta_out.at[2 + 2 * n], ts.at[6 + n], tr.at[6 + n], d))
    for n, d in enumerate(dests):
        share.append(send(dt.at[pl.ds(64 + 16 * n, 16)], dt_out.at[pl.ds(128 + 32 * n, 16)],
                          ts.at[2 + n], tr.at[2 + n], d))
    lax.fori_loop(0, 8, arrange, 0)
    ld = pltpu.make_async_copy(dt.at[pl.ds(0, 64)], dt_out.at[pl.ds(0, 64)], ls.at[4])
    ld.start()
    m1 = send(dt.at[pl.ds(0, 64)], dt_out.at[pl.ds(64, 64)], ts.at[1], tr.at[1], twin)

    lc.wait()
    for cp in first:
        cp.wait_recv()

    a = pl.ds(0, 2)
    b = pl.ds(2, 2)
    used = [0]

    def pass_on(ref, d):
        n = used[0]
        used[0] += 1
        return send(ref, ref, ss.at[n], sr.at[n], d)

    def spread_a(xs):
        return pass_on(q_out.at[y, a, xs], up), pass_on(q_out.at[y, a, xs], down)

    def spread_b(ys):
        return pass_on(q_out.at[ys, b, x], right), pass_on(q_out.at[ys, b, x], left)

    def relay_a(xs, pair):
        pair[0].wait_recv()
        f = pass_on(q_out.at[ym, 0, xs], up)
        pair[1].wait_recv()
        return f, pass_on(q_out.at[yp, 1, xs], down)

    def relay_b(ys, pair):
        pair[0].wait_recv()
        f = pass_on(q_out.at[ys, 2, xm], right)
        pair[1].wait_recv()
        return f, pass_on(q_out.at[ys, 3, xp], left)

    s0 = pass_on(q_out.at[y, a, x], right)
    s1 = pass_on(q_out.at[y, a, x], left)
    s2 = pass_on(q_out.at[y, b, x], up)
    s3 = pass_on(q_out.at[y, b, x], down)
    a0 = spread_a(x)
    b0 = spread_b(y)
    s0.wait_recv()
    s4 = pass_on(q_out.at[y, 0, xm], right)
    s1.wait_recv()
    s5 = pass_on(q_out.at[y, 1, xp], left)
    s2.wait_recv()
    s6 = pass_on(q_out.at[ym, 2, x], up)
    s3.wait_recv()
    s7 = pass_on(q_out.at[yp, 3, x], down)
    for n in range(4):
        share[n].wait_recv()
        m2 = meta_out.at[2 + 2 * n]
        share.append(send(m2, meta_out.at[3 + 2 * n], ts.at[14 + n], tr.at[14 + n], twin))
    a1 = spread_a(xm)
    a2 = spread_a(xp)
    b1 = spread_b(ym)
    b2 = spread_b(yp)
    s4.wait_recv()
    s5.wait_recv()
    a3 = spread_a(x2)
    s6.wait_recv()
    s7.wait_recv()
    b3 = spread_b(y2)
    for n in range(4):
        share[4 + n].wait_recv()
        share.append(send(dt_out.at[pl.ds(128 + 32 * n, 16)], dt_out.at[pl.ds(144 + 32 * n, 16)],
                          ts.at[10 + n], tr.at[10 + n], twin))
    last = share[8:]
    for xs, ys, pa, pb in ((x, y, a0, b0), (xm, ym, a1, b1), (xp, yp, a2, b2), (x2, y2, a3, b3)):
        last.extend(relay_a(xs, pa))
        last.extend(relay_b(ys, pb))
    for cp in [m0, m1] + last:
        cp.wait_recv()
    for cp in (lo, ld):
        cp.wait()
    for cp in waits:
        cp.wait_send()


def gather(queries, lengths, documents):
    hbm = pl.BlockSpec(memory_space=pltpu.HBM)
    free = pl.BlockSpec(memory_space=pl.ANY)
    return pl.pallas_call(
        gather_kernel,
        name="gather_queries",
        out_shape=(
            jax.ShapeDtypeStruct((4, 4, 4, 2, 64, 128), jnp.bfloat16),
            jax.ShapeDtypeStruct((256, CH, 128), jnp.bfloat16),
            jax.ShapeDtypeStruct((10, 8, 128), jnp.int32),
        ),
        in_specs=[hbm, hbm, hbm],
        out_specs=(free, free, free),
        scratch_shapes=[
            pltpu.VMEM((8, 16, 128), jnp.bfloat16),
            pltpu.VMEM((1, 128), jnp.int32),
            pltpu.VMEM((64, 128), jnp.float32),
            pltpu.VMEM((2, 64, 128), jnp.bfloat16),
            pltpu.VMEM((128, 64, 128), jnp.bfloat16),
            pltpu.VMEM((512, 128), jnp.float32),
            pltpu.VMEM((128, CH, 128), jnp.bfloat16),
            pltpu.VMEM((8, 128), jnp.int32),
            pltpu.SMEM((8, 128), jnp.int32),
            pltpu.SemaphoreType.DMA((7,)),
            pltpu.SemaphoreType.DMA((7,)),
            pltpu.SemaphoreType.DMA((40,)),
            pltpu.SemaphoreType.DMA((40,)),
            pltpu.SemaphoreType.DMA((18,)),
            pltpu.SemaphoreType.DMA((18,)),
            pltpu.SemaphoreType.DMA((8,)),
        ],
        compiler_params=pltpu.CompilerParams(collective_id=0, has_side_effects=True, vmem_limit_bytes=12 << 20),
    )(*[pltpu.with_memory_space_constraint(v, pltpu.HBM) for v in (queries, lengths, documents)])


def score_kernel(position, *refs):
    pl.run_scoped(
        functools.partial(score_body, position, *refs),
        *([pltpu.ACC(0)((CH, 256), jnp.float32)] * NS + [pltpu.ACC(1)((CH, 256), jnp.float32)] * NS),
    )


def around(idx):
    c, x, zl, y = idx % 2, (idx // 2) % 4, (idx // 8) % 4, idx // 32

    def at(y, x, c):
        return ((y * 4 + zl) * 4 + x) * 2 + c

    xp, xm, yp, ym = (x + 1) % 4, (x + 3) % 4, (y + 1) % 4, (y + 3) % 4
    return c, [[at(v, u, w) for w in (c, 1 - c)] for v, u in ((y, xm), (y, xp), (ym, x), (yp, x))]


def score_body(position, pat_ref, meta_vmem, rows, dt, out_ref, amax, total, stage, lists, steps, blocks, needs, sem, *accs):
    acc = (accs[:NS], accs[NS:])
    copy = pltpu.make_async_copy(meta_vmem.at[:, pl.ds(3, 1)], needs, sem)
    copy.start()
    stage[...] = jnp.zeros_like(stage)
    idx = position()
    c, near = around(idx)
    sides = [(idx, 0, 8, 0, 0), (idx + 1 - 2 * c, 8, 8, 1, 0)]
    for n in range(4):
        for o in range(2):
            sides.append((near[n][o], 16 + 4 * n + 2 * o, 2, 2 + 2 * n + o, 8 + 2 * n))

    def listing(k, n):
        t = jnp.int32(0)
        for col, here, groups, table, there in sides:
            def add(t, here=here, groups=groups, table=table, there=there):
                for g in range(groups):
                    for i in range(8):
                        lists[n, t + i] = (here + g) * 8 + i
                    t = t + needs[table, 0, (there + g) * 8]
                return t

            t = lax.cond(pat_ref[k, col] > 0, add, lambda t: t, t)

        @pl.when(t > 0)
        def _():
            end = lists[n, t - 1]
            for i in range(RUN):
                lists[n, t + i] = end
            steps[n] = (t + RUN - 1) // RUN
            blocks[n] = k

        return n + (t > 0).astype(jnp.int32)

    copy.wait()
    count = lax.fori_loop(0, 8, listing, jnp.int32(0))

    def weights(p):
        k = blocks[p]
        for m in range(2):
            w = []
            for half in range(2):
                low = (2 * half + m) * 32
                w.append(jnp.concatenate([rows[k, :, low + 16 * t:low + 16 * t + 16, :].reshape(128, 128) for t in range(2)], axis=0))
            pltpu.matmul_push_rhs(jnp.concatenate(w, axis=1), 0, m, transpose=True)

    def push(at, s, head=False):
        w = dt[at]
        for half in range(2):
            v = [w, jnp.zeros_like(w)]
            v = jnp.concatenate(v[::-1] if half else v, axis=1)
            for m in range(2):
                if head and half == 0:
                    pltpu.matmul_acc_lhs(acc[m][2 * s], v, load_staged_rhs=0)
                else:
                    pltpu.matmul_acc_lhs(acc[m][2 * s + half], v)

    def pop(at, s, tops):
        g = jnp.right_shift(at, 3)
        roof = jnp.where(jnp.bitwise_and(at, 7) == 0, -jnp.inf, jnp.inf).astype(jnp.float32)
        after = []
        for half in range(2):
            for m in range(2):
                r = pltpu.matmul_pop(acc[m][2 * s + half])
                r = jnp.max(r.reshape(8, 8, 256), axis=0)
                r = jnp.maximum(jnp.minimum(tops[2 * half + m], roof), r)
                amax[g, 2 * half + m] = r
                after.append(r)
        return after

    def close(p):
        value = (amax[:, 0] + amax[:, 1]) + (amax[:, 2] + amax[:, 3])
        total[p] = value[:, :, :128] + value[:, :, 128:]

    @pl.when(count > 0)
    def _():
        weights(0)

        def one_block(p, state):
            p0, last0, tops = state
            n = steps[p]
            olds = [lists[jnp.maximum(p0, 0), last0 * RUN + s] for s in range(RUN)]
            news = [lists[p, s] for s in range(RUN)]
            for s in range(RUN):
                tops = pop(olds[s], s, tops)
                push(news[s], s, head=s == 0)
            weights(jnp.minimum(p + 1, count - 1))
            close(jnp.where(p0 < 0, 8, p0))

            def further(m, tops):
                olds = [lists[p, (m - 1) * RUN + s] for s in range(RUN)]
                news = [lists[p, m * RUN + s] for s in range(RUN)]
                for s in range(RUN):
                    tops = pop(olds[s], s, tops)
                    push(news[s], s)
                return tops

            return p, n - 1, lax.fori_loop(1, n, further, tops)

        zero = jnp.int32(0)
        start = [jnp.full((8, 256), -jnp.inf, jnp.float32)] * 4
        p, last, tops = lax.fori_loop(0, count, one_block, (zero - 1, zero, start))
        for s in range(RUN):
            tops = pop(lists[p, last * RUN + s], s, tops)
        close(p)
        push(0, 0, head=True)
        for half in range(2):
            for m in range(2):
                pltpu.matmul_pop(acc[m][half])

        lane = lax.broadcasted_iota(jnp.int32, (32, 128), 1)

        def finish(p, _):
            k = blocks[p]
            flags = [pat_ref[k, side[0]] for side in sides]
            for part in range(2):
                on = jnp.zeros((32, 128), jnp.int32)
                for flag, (_, here, groups, _, _) in zip(flags, sides):
                    if here // 16 == part:
                        low = (here % 16) * 8
                        on = jnp.where((lane >= low) & (lane < low + groups * 8), flag, on)
                turned = total[p, part * 16:(part + 1) * 16].reshape(128, 128).T.reshape(8, 2, 8, 128)
                folded = turned[:, 0] + turned[:, 1]
                folded = (folded[:, 0:4] + folded[:, 4:8]).reshape(32, 128)
                stage[k // 4, pl.ds(pl.multiple_of((k % 4) * 32, 32), 32), part * 128:(part + 1) * 128] = (
                    jnp.where(on > 0, folded, 0.0))
            return 0

        lax.fori_loop(0, count, finish, 0)

    for side in range(2):
        for part in range(2):
            out_ref[side, part * 128:(part + 1) * 128] = stage[side, :, part * 128:(part + 1) * 128].T


def score(position, pattern, meta, rows, dt):
    smem = pl.BlockSpec(memory_space=pltpu.SMEM)
    vmem = pl.BlockSpec(memory_space=pltpu.VMEM)
    return pl.pallas_call(
        functools.partial(score_kernel, position),
        name="score_blocks",
        out_shape=jax.ShapeDtypeStruct((2, 256, 128), jnp.float32),
        in_specs=[smem, vmem, vmem, vmem],
        out_specs=vmem,
        scratch_shapes=[
            pltpu.VMEM((32, 4, 8, 256), jnp.float32),
            pltpu.VMEM((9, 32, 8, 128), jnp.float32),
            pltpu.VMEM((2, 128, 256), jnp.float32),
            pltpu.SMEM((8, 256 + NS), jnp.int32),
            pltpu.SMEM((8,), jnp.int32),
            pltpu.SMEM((8,), jnp.int32),
            pltpu.SMEM((10, 1, 128), jnp.int32),
            pltpu.SemaphoreType.DMA,
        ],
        compiler_params=pltpu.CompilerParams(vmem_limit_bytes=24 << 20),
    )(pattern, meta, rows, dt)


def swap_kernel(part_ref, meta_ref, out_ref, got, s_sem, r_sem):
    idx = lax.axis_index("docs")
    zh = lax.axis_index("pb")
    c, near = around(idx)
    twin = {"docs": idx + 1 - 2 * c, "pb": zh}
    partners = [{"docs": near[n][o], "pb": zh} for n in range(4) for o in range(2)]
    barrier = pltpu.get_barrier_semaphore()
    for d in partners + [twin]:
        pl.semaphore_signal(barrier, inc=1, device_id=d, device_id_type=MESH)
    pl.semaphore_wait(barrier, 9)
    copies = []
    for n in range(4):
        for o in range(2):
            q = 2 * n + o
            copies.append(pltpu.make_async_remote_copy(
                src_ref=part_ref.at[:, pl.ds(128 + 16 * q, 16)], dst_ref=got.at[c, :, pl.ds(64 + 16 * n, 16)],
                send_sem=s_sem.at[q], recv_sem=r_sem.at[q], device_id=partners[q], device_id_type=MESH))
    copies.append(pltpu.make_async_remote_copy(
        src_ref=part_ref.at[:, pl.ds(64, 64)], dst_ref=got.at[c, :, pl.ds(0, 64)],
        send_sem=s_sem.at[8], recv_sem=r_sem.at[8], device_id=twin, device_id_type=MESH))
    for cp in copies:
        cp.start()
    got[c, :, 0:64] = part_ref[:, 0:64]
    rank = jnp.broadcast_to(meta_ref[0, 1:2], (128, 128))
    for cp in copies:
        cp.wait_recv()
    for core in range(2):
        for half in range(2):
            back = jnp.take_along_axis(got[core, half].T, rank, axis=1).reshape(4, 8, 4, 128)
            for k in range(4):
                for h in range(8):
                    out_ref[(half * 4 + k) * 16 + h * 2 + core] = back[k, h]
    for cp in copies:
        cp.wait_send()


def swap(part, meta):
    vmem = pl.BlockSpec(memory_space=pltpu.VMEM)
    return pl.pallas_call(
        swap_kernel,
        name="swap_scores",
        out_shape=jax.ShapeDtypeStruct((128, 4, 128), jnp.float32),
        in_specs=[vmem, vmem],
        out_specs=vmem,
        scratch_shapes=[
            pltpu.VMEM((2, 2, 128, 128), jnp.float32),
            pltpu.SemaphoreType.DMA((9,)),
            pltpu.SemaphoreType.DMA((9,)),
        ],
        compiler_params=pltpu.CompilerParams(collective_id=1, has_side_effects=True, vmem_limit_bytes=4 << 20),
    )(part, meta)


def local(queries, documents, lengths, pattern):
    rows, dt, meta = gather(queries, lengths.reshape(1, 128), documents)
    part = score(lambda: lax.axis_index("docs"), pattern, meta, rows.reshape(8, 8, 128, 128), dt)
    return swap(part, meta)


def solution(mesh):
    return jax.shard_map(
        local,
        mesh=mesh,
        in_specs=(P("docs", "pb", None), P("docs", None, None), P("docs"), P()),
        out_specs=P(None, "pb", "docs"),
        check_vma=False,
    )
```

```python
import functools

import jax
import jax.numpy as jnp
from jax import lax
from jax.experimental import pallas as pl
from jax.experimental.pallas import tpu as pltpu
from jax.sharding import PartitionSpec as P

MESH = pl.DeviceIdType.MESH
CH = 64
NS = 12
RUN = NS // 2


def device(y, zl, x, c, h):
    return {"docs": ((y * 4 + zl) * 4 + x) * 2 + c, "pb": h}


def around(idx):
    c, x, zl, y = idx % 2, (idx // 2) % 4, (idx // 8) % 4, idx // 32

    def at(y, x, c):
        return ((y * 4 + zl) * 4 + x) * 2 + c

    xp, xm, yp, ym = (x + 1) % 4, (x + 3) % 4, (y + 1) % 4, (y + 3) % 4
    return c, [[at(v, u, w) for w in (c, 1 - c)] for v, u in ((y, xm), (y, xp), (ym, x), (yp, x))]


def sides_of(idx):
    c, near = around(idx)
    sides = [(idx, 0, 8, 0, 0), (idx + 1 - 2 * c, 8, 8, 1, 0)]
    for n in range(4):
        for o in range(2):
            sides.append((near[n][o], 16 + 4 * n + 2 * o, 2, 2 + 2 * n + o, 8 + 2 * n))
    return sides


def list_steps(idx, tables, pattern, plan):
    row = lax.broadcasted_iota(jnp.int32, (32, 128), 0)
    lane = lax.broadcasted_iota(jnp.int32, (32, 128), 1)
    col = jnp.zeros((32, 128), jnp.int32)
    first = jnp.zeros((32, 128), jnp.int32)
    values = jnp.zeros((32, 128), jnp.int32)
    for block, here, groups, table, there in sides_of(idx):
        mine = (row >= here) & (row < here + groups)
        col = jnp.where(mine, block, col)
        first = jnp.where(mine, (there + row - here) * 8, first)
        values = jnp.where(mine, jnp.broadcast_to(tables[table, 3:4], (32, 128)), values)
    need = jnp.sum(jnp.where(lane == first, values, 0), axis=1, keepdims=True)
    t = lax.broadcasted_iota(jnp.int32, (32, 384), 1)
    for k in range(8):
        flags = jnp.broadcast_to(pattern[k:k + 1], (32, 128))
        on = jnp.sum(jnp.where(lane == col, flags, 0), axis=1, keepdims=True)
        size = jnp.where(on > 0, need, 0)
        turned = jnp.sum(jnp.where(lane == row, size, 0), axis=0, keepdims=True)
        ends = jnp.sum(jnp.where(lane <= row, turned, 0), axis=1, keepdims=True)
        steps = jnp.sum(turned, axis=1, keepdims=True)
        place = jnp.minimum(t, steps - 1)
        listed = place[0:1] + jnp.sum(jnp.where(ends <= place, 8 - size, 0), axis=0, keepdims=True)
        plan[k:k + 1, 0:384] = listed
        plan[k:k + 1, 384:512] = jnp.broadcast_to(steps, (1, 128))


SHARES = (0, 2, 4, 6, 9, 11, 13, 15, 1, 14, 3, 12, 5, 10, 7, 8)


def placed(rank):
    group = rank // 8
    slot = jnp.zeros_like(rank)
    for n, g in enumerate(SHARES):
        slot = jnp.where(group == g, n, slot)
    return slot * 8 + rank % 8


def gather_kernel(q_hbm, len_hbm, d_hbm, pat_hbm, q_out, dt_out, meta_out, plan_out,
                  q_ref, len_ref, pat_ref, tables, plan, tmp, prep, docs, wide, dt, meta, meta_s, zs, zr, ss, sr, ts, tr, ls):
    loads = [pltpu.make_async_copy(src, dst, ls.at[5 + n])
             for n, (src, dst) in enumerate(((q_hbm, q_ref), (len_hbm, len_ref), (d_hbm, docs), (pat_hbm, pat_ref)))]
    for cp in loads:
        cp.start()
    idx = lax.axis_index("docs")
    zh = lax.axis_index("pb")
    c = idx % 2
    x = (idx // 2) % 4
    zl = (idx // 8) % 4
    y = idx // 32
    z = zh * 4 + zl
    xp, xm, yp, ym = (x + 1) % 4, (x + 3) % 4, (y + 1) % 4, (y + 3) % 4
    x2, y2 = (x + 2) % 4, (y + 2) % 4
    right, left = device(y, zl, xp, c, zh), device(y, zl, xm, c, zh)
    up, down = device(yp, zl, x, c, zh), device(ym, zl, x, c, zh)
    twin = device(y, zl, x, 1 - c, zh)
    column = []
    for s in (4, 3, 5, 2, 6, 1, 7):
        zt = (z + s) % 8
        column.append((zt // 4, device(y, zt % 4, x, c, zt // 4)))

    barrier = pltpu.get_barrier_semaphore()
    for d in [d for _, d in column] + [right, left, up, down, twin]:
        pl.semaphore_signal(barrier, inc=1, device_id=d, device_id_type=MESH)

    loads[0].wait()
    for h in range(2):
        for q in range(4):
            tmp[pl.ds(q, 16, stride=4), :] = q_ref[4 * h + q].astype(jnp.float32)
        prep[h] = tmp[...].astype(jnp.bfloat16)

    loads[1].wait()
    lanes = jnp.broadcast_to(len_ref[...], (128, 128))
    cols = lanes.T
    r = lax.broadcasted_iota(jnp.int32, (128, 128), 0)
    k = lax.broadcasted_iota(jnp.int32, (128, 128), 1)
    ahead_col = (lanes > cols) | ((lanes == cols) & (k < r))
    ahead_row = (cols > lanes) | ((cols == lanes) & (r < k))
    rank_col = placed(jnp.sum(jnp.where(ahead_col, 1, 0), axis=1, keepdims=True))
    rank_row = placed(jnp.sum(jnp.where(ahead_row, 1, 0), axis=0, keepdims=True))
    here = rank_col == k
    sizes = jnp.sum(jnp.where(here, cols, 0), axis=0, keepdims=True)
    meta[0:1] = sizes
    meta[1:2] = rank_row
    meta[2:3] = jnp.sum(jnp.where(here, r, 0), axis=0, keepdims=True)
    meta[3:4] = (sizes + 7) // 8
    meta[4:8] = jnp.zeros((4, 128), jnp.int32)
    lm = pltpu.make_async_copy(meta, meta_s, ls.at[2])
    lm.start()
    lm.wait()
    share = []
    loads[2].wait()

    def arrange(g, _):
        for i in range(8):
            rows = docs[jnp.bitwise_and(meta_s[2, g * 8 + i], 127)].astype(jnp.float32)
            slot = lax.broadcasted_iota(jnp.int32, rows.shape, 0)
            wide[pl.ds(i, 64, stride=8), :] = jnp.where(slot < meta_s[0, g * 8 + i], rows, rows[0:1])
        for i in range(8):
            dt[g * 8 + i] = wide[i * CH:(i + 1) * CH].astype(jnp.bfloat16)
        return 0

    lax.fori_loop(8, 16, arrange, 0)
    pl.semaphore_wait(barrier, 12)

    own = q_out.at[y, zl, x, zh]
    waits = []

    def send(src, dst, s_sem, r_sem, d):
        cp = pltpu.make_async_remote_copy(
            src_ref=src, dst_ref=dst, send_sem=s_sem, recv_sem=r_sem, device_id=d, device_id_type=MESH)
        cp.start()
        waits.append(cp)
        return cp

    first = [send(prep.at[ht], own, zs.at[s], zr.at[s], d) for s, (ht, d) in enumerate(column)]
    lc = pltpu.make_async_copy(prep.at[zh], own, ls.at[1])
    lc.start()

    dests = (right, left, up, down)
    lo = pltpu.make_async_copy(meta, meta_out.at[0], ls.at[3])
    lo.start()
    m0 = send(meta, meta_out.at[1], ts.at[0], tr.at[0], twin)
    for n, d in enumerate(dests):
        share.append(send(meta, meta_out.at[2 + 2 * n], ts.at[6 + n], tr.at[6 + n], d))
    for n, d in enumerate(dests):
        share.append(send(dt.at[pl.ds(64 + 16 * n, 16)], dt_out.at[pl.ds(128 + 32 * n, 16)],
                          ts.at[2 + n], tr.at[2 + n], d))
    lax.fori_loop(0, 8, arrange, 0)
    ld = pltpu.make_async_copy(dt.at[pl.ds(0, 64)], dt_out.at[pl.ds(0, 64)], ls.at[4])
    ld.start()
    m1 = send(dt.at[pl.ds(0, 64)], dt_out.at[pl.ds(64, 64)], ts.at[1], tr.at[1], twin)

    lc.wait()
    for cp in first:
        cp.wait_recv()

    a = pl.ds(0, 2)
    b = pl.ds(2, 2)
    used = [0]

    def pass_on(ref, d):
        n = used[0]
        used[0] += 1
        return send(ref, ref, ss.at[n], sr.at[n], d)

    def spread_a(xs):
        return pass_on(q_out.at[y, a, xs], up), pass_on(q_out.at[y, a, xs], down)

    def spread_b(ys):
        return pass_on(q_out.at[ys, b, x], right), pass_on(q_out.at[ys, b, x], left)

    def relay_a(xs, pair):
        pair[0].wait_recv()
        f = pass_on(q_out.at[ym, 0, xs], up)
        pair[1].wait_recv()
        return f, pass_on(q_out.at[yp, 1, xs], down)

    def relay_b(ys, pair):
        pair[0].wait_recv()
        f = pass_on(q_out.at[ys, 2, xm], right)
        pair[1].wait_recv()
        return f, pass_on(q_out.at[ys, 3, xp], left)

    s0 = pass_on(q_out.at[y, a, x], right)
    s1 = pass_on(q_out.at[y, a, x], left)
    s2 = pass_on(q_out.at[y, b, x], up)
    s3 = pass_on(q_out.at[y, b, x], down)
    a0 = spread_a(x)
    b0 = spread_b(y)
    s0.wait_recv()
    s4 = pass_on(q_out.at[y, 0, xm], right)
    s1.wait_recv()
    s5 = pass_on(q_out.at[y, 1, xp], left)
    s2.wait_recv()
    s6 = pass_on(q_out.at[ym, 2, x], up)
    s3.wait_recv()
    s7 = pass_on(q_out.at[yp, 3, x], down)
    for n in range(4):
        share[n].wait_recv()
        m2 = meta_out.at[2 + 2 * n]
        share.append(send(m2, meta_out.at[3 + 2 * n], ts.at[14 + n], tr.at[14 + n], twin))
    a1 = spread_a(xm)
    a2 = spread_a(xp)
    b1 = spread_b(ym)
    b2 = spread_b(yp)
    s4.wait_recv()
    s5.wait_recv()
    a3 = spread_a(x2)
    s6.wait_recv()
    s7.wait_recv()
    b3 = spread_b(y2)
    for n in range(4):
        share[4 + n].wait_recv()
        share.append(send(dt_out.at[pl.ds(128 + 32 * n, 16)], dt_out.at[pl.ds(144 + 32 * n, 16)],
                          ts.at[10 + n], tr.at[10 + n], twin))
    last = share[12:]
    for xs, ys, pa, pb in ((x, y, a0, b0), (xm, ym, a1, b1), (xp, yp, a2, b2), (x2, y2, a3, b3)):
        last.extend(relay_a(xs, pa))
        last.extend(relay_b(ys, pb))
    for cp in [m0] + share[8:12]:
        cp.wait_recv()
    lt = pltpu.make_async_copy(meta_out, tables, ls.at[9])
    lo.wait()
    lt.start()
    loads[3].wait()
    lt.wait()
    list_steps(idx, tables, pat_ref, plan)
    lp = pltpu.make_async_copy(plan, plan_out, ls.at[10])
    lp.start()
    for cp in [m1] + last:
        cp.wait_recv()
    for cp in (ld, lp):
        cp.wait()
    for cp in waits:
        cp.wait_send()


def gather(queries, lengths, documents, pattern):
    hbm = pl.BlockSpec(memory_space=pltpu.HBM)
    free = pl.BlockSpec(memory_space=pl.ANY)
    return pl.pallas_call(
        gather_kernel,
        name="gather_queries",
        out_shape=(
            jax.ShapeDtypeStruct((4, 4, 4, 2, 64, 128), jnp.bfloat16),
            jax.ShapeDtypeStruct((256, CH, 128), jnp.bfloat16),
            jax.ShapeDtypeStruct((10, 8, 128), jnp.int32),
            jax.ShapeDtypeStruct((8, 512), jnp.int32),
        ),
        in_specs=[hbm, hbm, hbm, hbm],
        out_specs=(free, free, free, free),
        scratch_shapes=[
            pltpu.VMEM((8, 16, 128), jnp.bfloat16),
            pltpu.VMEM((1, 128), jnp.int32),
            pltpu.VMEM((8, 128), jnp.int32),
            pltpu.VMEM((10, 8, 128), jnp.int32),
            pltpu.VMEM((8, 512), jnp.int32),
            pltpu.VMEM((64, 128), jnp.float32),
            pltpu.VMEM((2, 64, 128), jnp.bfloat16),
            pltpu.VMEM((128, 64, 128), jnp.bfloat16),
            pltpu.VMEM((512, 128), jnp.float32),
            pltpu.VMEM((128, CH, 128), jnp.bfloat16),
            pltpu.VMEM((8, 128), jnp.int32),
            pltpu.SMEM((8, 128), jnp.int32),
            pltpu.SemaphoreType.DMA((7,)),
            pltpu.SemaphoreType.DMA((7,)),
            pltpu.SemaphoreType.DMA((40,)),
            pltpu.SemaphoreType.DMA((40,)),
            pltpu.SemaphoreType.DMA((18,)),
            pltpu.SemaphoreType.DMA((18,)),
            pltpu.SemaphoreType.DMA((11,)),
        ],
        compiler_params=pltpu.CompilerParams(collective_id=0, has_side_effects=True, vmem_limit_bytes=12 << 20),
    )(*[pltpu.with_memory_space_constraint(v, pltpu.HBM) for v in (queries, lengths, documents, pattern)])


def score_kernel(position, *refs):
    pl.run_scoped(
        functools.partial(score_body, position, *refs),
        *([pltpu.ACC(0)((CH, 256), jnp.float32)] * NS + [pltpu.ACC(1)((CH, 256), jnp.float32)] * NS),
    )


def score_body(position, pat_ref, plan, rows, dt, out_ref, amax, total, stage, steps, blocks, *accs):
    acc = (accs[:NS], accs[NS:])
    sides = sides_of(position())

    def active(k, n):
        t = plan[k, 384]

        @pl.when(t > 0)
        def _():
            blocks[n] = k
            steps[n] = (t + RUN - 1) // RUN

        return n + (t > 0).astype(jnp.int32)

    count = lax.fori_loop(0, 8, active, jnp.int32(0))
    stage[...] = jnp.zeros_like(stage)

    def weights(p):
        k = blocks[p]
        for m in range(2):
            w = []
            for half in range(2):
                low = (2 * half + m) * 32
                w.append(jnp.concatenate([rows[k, :, low + 16 * t:low + 16 * t + 16, :].reshape(128, 128) for t in range(2)], axis=0))
            pltpu.matmul_push_rhs(jnp.concatenate(w, axis=1), 0, m, transpose=True)

    def push(at, s, head=False):
        w = dt[at]
        for half in range(2):
            v = [w, jnp.zeros_like(w)]
            v = jnp.concatenate(v[::-1] if half else v, axis=1)
            for m in range(2):
                if head and half == 0:
                    pltpu.matmul_acc_lhs(acc[m][2 * s], v, load_staged_rhs=0)
                else:
                    pltpu.matmul_acc_lhs(acc[m][2 * s + half], v)

    def pop(at, s, tops):
        g = jnp.right_shift(at, 3)
        roof = jnp.where(jnp.bitwise_and(at, 7) == 0, -jnp.inf, jnp.inf).astype(jnp.float32)
        after = []
        for half in range(2):
            for m in range(2):
                r = pltpu.matmul_pop(acc[m][2 * s + half])
                r = jnp.max(r.reshape(8, 8, 256), axis=0)
                r = jnp.maximum(jnp.minimum(tops[2 * half + m], roof), r)
                amax[g, 2 * half + m] = r
                after.append(r)
        return after

    def close(p):
        value = (amax[:, 0] + amax[:, 1]) + (amax[:, 2] + amax[:, 3])
        total[p] = value[:, :, :128] + value[:, :, 128:]

    @pl.when(count > 0)
    def _():
        weights(0)

        def one_block(p, state):
            p0, last0, tops = state
            n = steps[p]
            k, k0 = blocks[p], blocks[jnp.maximum(p0, 0)]
            olds = [plan[k0, last0 * RUN + s] for s in range(RUN)]
            news = [plan[k, s] for s in range(RUN)]
            for s in range(RUN):
                tops = pop(olds[s], s, tops)
                push(news[s], s, head=s == 0)
            weights(jnp.minimum(p + 1, count - 1))
            close(jnp.where(p0 < 0, 8, p0))

            def further(m, tops):
                olds = [plan[k, (m - 1) * RUN + s] for s in range(RUN)]
                news = [plan[k, m * RUN + s] for s in range(RUN)]
                for s in range(RUN):
                    tops = pop(olds[s], s, tops)
                    push(news[s], s)
                return tops

            return p, n - 1, lax.fori_loop(1, n, further, tops)

        zero = jnp.int32(0)
        start = [jnp.full((8, 256), -jnp.inf, jnp.float32)] * 4
        p, last, tops = lax.fori_loop(0, count, one_block, (zero - 1, zero, start))
        for s in range(RUN):
            tops = pop(plan[blocks[p], last * RUN + s], s, tops)
        close(p)
        push(0, 0, head=True)
        for half in range(2):
            for m in range(2):
                pltpu.matmul_pop(acc[m][half])

        lane = lax.broadcasted_iota(jnp.int32, (32, 128), 1)

        def finish(p, _):
            k = blocks[p]
            flags = [pat_ref[k, side[0]] for side in sides]
            for part in range(2):
                on = jnp.zeros((32, 128), jnp.int32)
                for flag, (_, here, groups, _, _) in zip(flags, sides):
                    if here // 16 == part:
                        low = (here % 16) * 8
                        on = jnp.where((lane >= low) & (lane < low + groups * 8), flag, on)
                turned = total[p, part * 16:(part + 1) * 16].reshape(128, 128).T.reshape(8, 2, 8, 128)
                folded = turned[:, 0] + turned[:, 1]
                folded = (folded[:, 0:4] + folded[:, 4:8]).reshape(32, 128)
                stage[k // 4, pl.ds(pl.multiple_of((k % 4) * 32, 32), 32), part * 128:(part + 1) * 128] = (
                    jnp.where(on > 0, folded, 0.0))
            return 0

        lax.fori_loop(0, count, finish, 0)

    for side in range(2):
        for part in range(2):
            out_ref[side, part * 128:(part + 1) * 128] = stage[side, :, part * 128:(part + 1) * 128].T


def score(position, pattern, plan, rows, dt):
    smem = pl.BlockSpec(memory_space=pltpu.SMEM)
    vmem = pl.BlockSpec(memory_space=pltpu.VMEM)
    return pl.pallas_call(
        functools.partial(score_kernel, position),
        name="score_blocks",
        out_shape=jax.ShapeDtypeStruct((2, 256, 128), jnp.float32),
        in_specs=[smem, smem, vmem, vmem],
        out_specs=vmem,
        scratch_shapes=[
            pltpu.VMEM((32, 4, 8, 256), jnp.float32),
            pltpu.VMEM((9, 32, 8, 128), jnp.float32),
            pltpu.VMEM((2, 128, 256), jnp.float32),
            pltpu.SMEM((8,), jnp.int32),
            pltpu.SMEM((8,), jnp.int32),
        ],
        compiler_params=pltpu.CompilerParams(vmem_limit_bytes=24 << 20),
    )(pattern, plan, rows, dt)


def swap_kernel(part_ref, meta_ref, out_ref, got, s_sem, r_sem):
    idx = lax.axis_index("docs")
    zh = lax.axis_index("pb")
    c, near = around(idx)
    twin = {"docs": idx + 1 - 2 * c, "pb": zh}
    partners = [{"docs": near[n][o], "pb": zh} for n in range(4) for o in range(2)]
    barrier = pltpu.get_barrier_semaphore()
    for d in partners + [twin]:
        pl.semaphore_signal(barrier, inc=1, device_id=d, device_id_type=MESH)
    pl.semaphore_wait(barrier, 9)
    copies = []
    for n in range(4):
        for o in range(2):
            q = 2 * n + o
            copies.append(pltpu.make_async_remote_copy(
                src_ref=part_ref.at[:, pl.ds(128 + 16 * q, 16)], dst_ref=got.at[c, :, pl.ds(64 + 16 * n, 16)],
                send_sem=s_sem.at[q], recv_sem=r_sem.at[q], device_id=partners[q], device_id_type=MESH))
    copies.append(pltpu.make_async_remote_copy(
        src_ref=part_ref.at[:, pl.ds(64, 64)], dst_ref=got.at[c, :, pl.ds(0, 64)],
        send_sem=s_sem.at[8], recv_sem=r_sem.at[8], device_id=twin, device_id_type=MESH))
    for cp in copies:
        cp.start()
    got[c, :, 0:64] = part_ref[:, 0:64]
    rank = jnp.broadcast_to(meta_ref[0, 1:2], (128, 128))
    for cp in copies:
        cp.wait_recv()
    for core in range(2):
        for half in range(2):
            back = jnp.take_along_axis(got[core, half].T, rank, axis=1).reshape(4, 8, 4, 128)
            for k in range(4):
                for h in range(8):
                    out_ref[(half * 4 + k) * 16 + h * 2 + core] = back[k, h]
    for cp in copies:
        cp.wait_send()


def swap(part, meta):
    vmem = pl.BlockSpec(memory_space=pltpu.VMEM)
    return pl.pallas_call(
        swap_kernel,
        name="swap_scores",
        out_shape=jax.ShapeDtypeStruct((128, 4, 128), jnp.float32),
        in_specs=[vmem, vmem],
        out_specs=vmem,
        scratch_shapes=[
            pltpu.VMEM((2, 2, 128, 128), jnp.float32),
            pltpu.SemaphoreType.DMA((9,)),
            pltpu.SemaphoreType.DMA((9,)),
        ],
        compiler_params=pltpu.CompilerParams(collective_id=1, has_side_effects=True, vmem_limit_bytes=4 << 20),
    )(part, meta)


def local(queries, documents, lengths, pattern):
    rows, dt, meta, plan = gather(queries, lengths.reshape(1, 128), documents, pattern)
    part = score(lambda: lax.axis_index("docs"), pattern, plan, rows.reshape(8, 8, 128, 128), dt)
    return swap(part, meta)


def solution(mesh):
    return jax.shard_map(
        local,
        mesh=mesh,
        in_specs=(P("docs", "pb", None), P("docs", None, None), P("docs"), P()),
        out_specs=P(None, "pb", "docs"),
        check_vma=False,
    )
```

```python
import functools

import jax
import jax.numpy as jnp
from jax import lax
from jax.experimental import pallas as pl
from jax.experimental.pallas import tpu as pltpu
from jax.sharding import PartitionSpec as P

MESH = pl.DeviceIdType.MESH
CH = 64
NS = 12
RUN = NS // 2


def device(y, zl, x, c, h):
    return {"docs": ((y * 4 + zl) * 4 + x) * 2 + c, "pb": h}


def around(idx):
    c, x, zl, y = idx % 2, (idx // 2) % 4, (idx // 8) % 4, idx // 32

    def at(y, x, c):
        return ((y * 4 + zl) * 4 + x) * 2 + c

    xp, xm, yp, ym = (x + 1) % 4, (x + 3) % 4, (y + 1) % 4, (y + 3) % 4
    return c, [[at(v, u, w) for w in (c, 1 - c)] for v, u in ((y, xm), (y, xp), (ym, x), (yp, x))]


def sides_of(idx):
    c, near = around(idx)
    sides = [(idx, 0, 8, 0, 0), (idx + 1 - 2 * c, 8, 8, 1, 0)]
    for n in range(4):
        for o in range(2):
            sides.append((near[n][o], 16 + 4 * n + 2 * o, 2, 2 + 2 * n + o, 8 + 2 * n))
    return sides


def list_steps(idx, tables, pattern, plan):
    row = lax.broadcasted_iota(jnp.int32, (32, 128), 0)
    lane = lax.broadcasted_iota(jnp.int32, (32, 128), 1)
    col = jnp.zeros((32, 128), jnp.int32)
    first = jnp.zeros((32, 128), jnp.int32)
    values = jnp.zeros((32, 128), jnp.int32)
    for block, here, groups, table, there in sides_of(idx):
        mine = (row >= here) & (row < here + groups)
        col = jnp.where(mine, block, col)
        first = jnp.where(mine, (there + row - here) * 8, first)
        values = jnp.where(mine, jnp.broadcast_to(tables[table, 3:4], (32, 128)), values)
    need = jnp.sum(jnp.where(lane == first, values, 0), axis=1, keepdims=True)
    t = lax.broadcasted_iota(jnp.int32, (32, 384), 1)
    for k in range(8):
        flags = jnp.broadcast_to(pattern[k:k + 1], (32, 128))
        on = jnp.sum(jnp.where(lane == col, flags, 0), axis=1, keepdims=True)
        size = jnp.where(on > 0, need, 0)
        turned = jnp.sum(jnp.where(lane == row, size, 0), axis=0, keepdims=True)
        ends = jnp.sum(jnp.where(lane <= row, turned, 0), axis=1, keepdims=True)
        steps = jnp.sum(turned, axis=1, keepdims=True)
        place = jnp.minimum(t, steps - 1)
        listed = place[0:1] + jnp.sum(jnp.where(ends <= place, 8 - size, 0), axis=0, keepdims=True)
        plan[k:k + 1, 0:384] = listed
        plan[k:k + 1, 384:512] = jnp.broadcast_to(steps, (1, 128))


SHARES = (0, 2, 4, 6, 9, 11, 13, 15, 1, 14, 3, 12, 5, 10, 7, 8)


def placed(rank):
    group = rank // 8
    slot = jnp.zeros_like(rank)
    for n, g in enumerate(SHARES):
        slot = jnp.where(group == g, n, slot)
    return slot * 8 + rank % 8


def gather_kernel(q_hbm, len_hbm, d_hbm, pat_hbm, q_out, dt_out, meta_out, plan_out,
                  q_ref, len_ref, pat_ref, tables, plan, tmp, prep, docs, wide, dt, meta, meta_s, zs, zr, ss, sr, ts, tr, ls):
    loads = [pltpu.make_async_copy(src, dst, ls.at[5 + n])
             for n, (src, dst) in enumerate(((q_hbm, q_ref), (len_hbm, len_ref), (d_hbm, docs), (pat_hbm, pat_ref)))]
    for cp in loads:
        cp.start()
    idx = lax.axis_index("docs")
    zh = lax.axis_index("pb")
    c = idx % 2
    x = (idx // 2) % 4
    zl = (idx // 8) % 4
    y = idx // 32
    z = zh * 4 + zl
    xp, xm, yp, ym = (x + 1) % 4, (x + 3) % 4, (y + 1) % 4, (y + 3) % 4
    x2, y2 = (x + 2) % 4, (y + 2) % 4
    right, left = device(y, zl, xp, c, zh), device(y, zl, xm, c, zh)
    up, down = device(yp, zl, x, c, zh), device(ym, zl, x, c, zh)
    twin = device(y, zl, x, 1 - c, zh)
    column = []
    for s in (4, 3, 5, 2, 6, 1, 7):
        zt = (z + s) % 8
        column.append((zt // 4, device(y, zt % 4, x, c, zt // 4)))

    barrier = pltpu.get_barrier_semaphore()
    for d in [d for _, d in column] + [right, left, up, down, twin]:
        pl.semaphore_signal(barrier, inc=1, device_id=d, device_id_type=MESH)

    loads[0].wait()
    for h in range(2):
        for q in range(4):
            tmp[pl.ds(q, 16, stride=4), :] = q_ref[4 * h + q].astype(jnp.float32)
        prep[h] = tmp[...].astype(jnp.bfloat16)

    loads[1].wait()
    lanes = jnp.broadcast_to(len_ref[...], (128, 128))
    cols = lanes.T
    r = lax.broadcasted_iota(jnp.int32, (128, 128), 0)
    k = lax.broadcasted_iota(jnp.int32, (128, 128), 1)
    ahead_col = (lanes > cols) | ((lanes == cols) & (k < r))
    ahead_row = (cols > lanes) | ((cols == lanes) & (r < k))
    rank_col = placed(jnp.sum(jnp.where(ahead_col, 1, 0), axis=1, keepdims=True))
    rank_row = placed(jnp.sum(jnp.where(ahead_row, 1, 0), axis=0, keepdims=True))
    here = rank_col == k
    sizes = jnp.sum(jnp.where(here, cols, 0), axis=0, keepdims=True)
    meta[0:1] = sizes
    meta[1:2] = rank_row
    meta[2:3] = jnp.sum(jnp.where(here, r, 0), axis=0, keepdims=True)
    meta[3:4] = (sizes + 7) // 8
    meta[4:8] = jnp.zeros((4, 128), jnp.int32)
    lm = pltpu.make_async_copy(meta, meta_s, ls.at[2])
    lm.start()
    lm.wait()
    share = []
    loads[2].wait()

    def arrange(g, _):
        for i in range(8):
            rows = docs[jnp.bitwise_and(meta_s[2, g * 8 + i], 127)].astype(jnp.float32)
            slot = lax.broadcasted_iota(jnp.int32, rows.shape, 0)
            wide[pl.ds(i, 64, stride=8), :] = jnp.where(slot < meta_s[0, g * 8 + i], rows, rows[0:1])
        for i in range(8):
            dt[g * 8 + i] = wide[i * CH:(i + 1) * CH].astype(jnp.bfloat16)
        return 0

    lax.fori_loop(8, 16, arrange, 0)
    pl.semaphore_wait(barrier, 12)

    own = q_out.at[y, zl, x, zh]
    waits = []

    def send(src, dst, s_sem, r_sem, d):
        cp = pltpu.make_async_remote_copy(
            src_ref=src, dst_ref=dst, send_sem=s_sem, recv_sem=r_sem, device_id=d, device_id_type=MESH)
        cp.start()
        waits.append(cp)
        return cp

    first = [send(prep.at[ht], own, zs.at[s], zr.at[s], d) for s, (ht, d) in enumerate(column)]
    lc = pltpu.make_async_copy(prep.at[zh], own, ls.at[1])
    lc.start()

    dests = (right, left, up, down)
    lo = pltpu.make_async_copy(meta, meta_out.at[0], ls.at[3])
    lo.start()
    m0 = send(meta, meta_out.at[1], ts.at[0], tr.at[0], twin)
    for n, d in enumerate(dests):
        share.append(send(meta, meta_out.at[2 + 2 * n], ts.at[6 + n], tr.at[6 + n], d))
    for n, d in enumerate(dests):
        share.append(send(dt.at[pl.ds(64 + 16 * n, 16)], dt_out.at[pl.ds(128 + 32 * n, 16)],
                          ts.at[2 + n], tr.at[2 + n], d))
    lax.fori_loop(0, 8, arrange, 0)
    ld = pltpu.make_async_copy(dt.at[pl.ds(0, 64)], dt_out.at[pl.ds(0, 64)], ls.at[4])
    ld.start()
    m1 = send(dt.at[pl.ds(0, 64)], dt_out.at[pl.ds(64, 64)], ts.at[1], tr.at[1], twin)

    lc.wait()
    for cp in first:
        cp.wait_recv()

    a = pl.ds(0, 2)
    b = pl.ds(2, 2)
    used = [0]

    def pass_on(ref, d):
        n = used[0]
        used[0] += 1
        return send(ref, ref, ss.at[n], sr.at[n], d)

    def spread_a(xs):
        return pass_on(q_out.at[y, a, xs], up), pass_on(q_out.at[y, a, xs], down)

    def spread_b(ys):
        return pass_on(q_out.at[ys, b, x], right), pass_on(q_out.at[ys, b, x], left)

    def relay_a(xs, pair):
        pair[0].wait_recv()
        f = pass_on(q_out.at[ym, 0, xs], up)
        pair[1].wait_recv()
        return f, pass_on(q_out.at[yp, 1, xs], down)

    def relay_b(ys, pair):
        pair[0].wait_recv()
        f = pass_on(q_out.at[ys, 2, xm], right)
        pair[1].wait_recv()
        return f, pass_on(q_out.at[ys, 3, xp], left)

    s0 = pass_on(q_out.at[y, a, x], right)
    s1 = pass_on(q_out.at[y, a, x], left)
    s2 = pass_on(q_out.at[y, b, x], up)
    s3 = pass_on(q_out.at[y, b, x], down)
    a0 = spread_a(x)
    b0 = spread_b(y)
    s0.wait_recv()
    s4 = pass_on(q_out.at[y, 0, xm], right)
    s1.wait_recv()
    s5 = pass_on(q_out.at[y, 1, xp], left)
    s2.wait_recv()
    s6 = pass_on(q_out.at[ym, 2, x], up)
    s3.wait_recv()
    s7 = pass_on(q_out.at[yp, 3, x], down)
    for n in range(4):
        share[n].wait_recv()
        m2 = meta_out.at[2 + 2 * n]
        share.append(send(m2, meta_out.at[3 + 2 * n], ts.at[14 + n], tr.at[14 + n], twin))
    a1 = spread_a(xm)
    a2 = spread_a(xp)
    b1 = spread_b(ym)
    b2 = spread_b(yp)
    early = list(relay_a(x, a0)) + list(relay_b(y, b0))
    s4.wait_recv()
    s5.wait_recv()
    a3 = spread_a(x2)
    s6.wait_recv()
    s7.wait_recv()
    b3 = spread_b(y2)
    last = early
    for xs, ys, pa, pb in ((xm, ym, a1, b1), (xp, yp, a2, b2), (x2, y2, a3, b3)):
        last.extend(relay_a(xs, pa))
        last.extend(relay_b(ys, pb))
        if xs is xm:
            for n in range(4):
                share[4 + n].wait_recv()
                share.append(send(dt_out.at[pl.ds(128 + 32 * n, 16)], dt_out.at[pl.ds(144 + 32 * n, 16)],
                                  ts.at[10 + n], tr.at[10 + n], twin))
    for cp in [m0] + share[8:12]:
        cp.wait_recv()
    lt = pltpu.make_async_copy(meta_out, tables, ls.at[9])
    lo.wait()
    lt.start()
    loads[3].wait()
    lt.wait()
    list_steps(idx, tables, pat_ref, plan)
    lp = pltpu.make_async_copy(plan, plan_out, ls.at[10])
    lp.start()
    for cp in [m1] + share[12:] + last:
        cp.wait_recv()
    for cp in (ld, lp):
        cp.wait()
    for cp in waits:
        cp.wait_send()


def gather(queries, lengths, documents, pattern):
    hbm = pl.BlockSpec(memory_space=pltpu.HBM)
    free = pl.BlockSpec(memory_space=pl.ANY)
    return pl.pallas_call(
        gather_kernel,
        name="gather_queries",
        out_shape=(
            jax.ShapeDtypeStruct((4, 4, 4, 2, 64, 128), jnp.bfloat16),
            jax.ShapeDtypeStruct((256, CH, 128), jnp.bfloat16),
            jax.ShapeDtypeStruct((10, 8, 128), jnp.int32),
            jax.ShapeDtypeStruct((8, 512), jnp.int32),
        ),
        in_specs=[hbm, hbm, hbm, hbm],
        out_specs=(free, free, free, free),
        scratch_shapes=[
            pltpu.VMEM((8, 16, 128), jnp.bfloat16),
            pltpu.VMEM((1, 128), jnp.int32),
            pltpu.VMEM((8, 128), jnp.int32),
            pltpu.VMEM((10, 8, 128), jnp.int32),
            pltpu.VMEM((8, 512), jnp.int32),
            pltpu.VMEM((64, 128), jnp.float32),
            pltpu.VMEM((2, 64, 128), jnp.bfloat16),
            pltpu.VMEM((128, 64, 128), jnp.bfloat16),
            pltpu.VMEM((512, 128), jnp.float32),
            pltpu.VMEM((128, CH, 128), jnp.bfloat16),
            pltpu.VMEM((8, 128), jnp.int32),
            pltpu.SMEM((8, 128), jnp.int32),
            pltpu.SemaphoreType.DMA((7,)),
            pltpu.SemaphoreType.DMA((7,)),
            pltpu.SemaphoreType.DMA((40,)),
            pltpu.SemaphoreType.DMA((40,)),
            pltpu.SemaphoreType.DMA((18,)),
            pltpu.SemaphoreType.DMA((18,)),
            pltpu.SemaphoreType.DMA((11,)),
        ],
        compiler_params=pltpu.CompilerParams(collective_id=0, has_side_effects=True, vmem_limit_bytes=12 << 20),
    )(*[pltpu.with_memory_space_constraint(v, pltpu.HBM) for v in (queries, lengths, documents, pattern)])


def score_kernel(position, *refs):
    pl.run_scoped(
        functools.partial(score_body, position, *refs),
        *([pltpu.ACC(0)((CH, 256), jnp.float32)] * NS + [pltpu.ACC(1)((CH, 256), jnp.float32)] * NS),
    )


def score_body(position, pat_ref, plan, rows, dt, out_ref, amax, total, stage, steps, blocks, *accs):
    acc = (accs[:NS], accs[NS:])
    sides = sides_of(position())

    def active(k, n):
        t = plan[k, 384]

        @pl.when(t > 0)
        def _():
            blocks[n] = k
            steps[n] = (t + RUN - 1) // RUN

        return n + (t > 0).astype(jnp.int32)

    count = lax.fori_loop(0, 8, active, jnp.int32(0))
    stage[...] = jnp.zeros_like(stage)

    def weights(p):
        k = blocks[p]
        for m in range(2):
            w = []
            for half in range(2):
                low = (2 * half + m) * 32
                w.append(jnp.concatenate([rows[k, :, low + 16 * t:low + 16 * t + 16, :].reshape(128, 128) for t in range(2)], axis=0))
            pltpu.matmul_push_rhs(jnp.concatenate(w, axis=1), 0, m, transpose=True)

    def push(at, s, head=False):
        w = dt[at]
        for half in range(2):
            v = [w, jnp.zeros_like(w)]
            v = jnp.concatenate(v[::-1] if half else v, axis=1)
            for m in range(2):
                if head and half == 0:
                    pltpu.matmul_acc_lhs(acc[m][2 * s], v, load_staged_rhs=0)
                else:
                    pltpu.matmul_acc_lhs(acc[m][2 * s + half], v)

    def pop(at, s, tops):
        g = jnp.right_shift(at, 3)
        roof = jnp.where(jnp.bitwise_and(at, 7) == 0, -jnp.inf, jnp.inf).astype(jnp.float32)
        after = []
        for half in range(2):
            for m in range(2):
                r = pltpu.matmul_pop(acc[m][2 * s + half])
                r = jnp.max(r.reshape(8, 8, 256), axis=0)
                r = jnp.maximum(jnp.minimum(tops[2 * half + m], roof), r)
                amax[g, 2 * half + m] = r
                after.append(r)
        return after

    def close(p):
        value = (amax[:, 0] + amax[:, 1]) + (amax[:, 2] + amax[:, 3])
        total[p] = value[:, :, :128] + value[:, :, 128:]

    @pl.when(count > 0)
    def _():
        weights(0)

        def one_block(p, state):
            p0, last0, tops = state
            n = steps[p]
            k, k0 = blocks[p], blocks[jnp.maximum(p0, 0)]
            olds = [plan[k0, last0 * RUN + s] for s in range(RUN)]
            news = [plan[k, s] for s in range(RUN)]
            for s in range(RUN):
                tops = pop(olds[s], s, tops)
                push(news[s], s, head=s == 0)
            weights(jnp.minimum(p + 1, count - 1))
            close(jnp.where(p0 < 0, 8, p0))

            def further(m, tops):
                olds = [plan[k, (m - 1) * RUN + s] for s in range(RUN)]
                news = [plan[k, m * RUN + s] for s in range(RUN)]
                for s in range(RUN):
                    tops = pop(olds[s], s, tops)
                    push(news[s], s)
                return tops

            return p, n - 1, lax.fori_loop(1, n, further, tops)

        zero = jnp.int32(0)
        start = [jnp.full((8, 256), -jnp.inf, jnp.float32)] * 4
        p, last, tops = lax.fori_loop(0, count, one_block, (zero - 1, zero, start))
        for s in range(RUN):
            tops = pop(plan[blocks[p], last * RUN + s], s, tops)
        close(p)
        push(0, 0, head=True)
        for half in range(2):
            for m in range(2):
                pltpu.matmul_pop(acc[m][half])

        lane = lax.broadcasted_iota(jnp.int32, (32, 128), 1)

        def finish(p, _):
            k = blocks[p]
            flags = [pat_ref[k, side[0]] for side in sides]
            for part in range(2):
                on = jnp.zeros((32, 128), jnp.int32)
                for flag, (_, here, groups, _, _) in zip(flags, sides):
                    if here // 16 == part:
                        low = (here % 16) * 8
                        on = jnp.where((lane >= low) & (lane < low + groups * 8), flag, on)
                turned = total[p, part * 16:(part + 1) * 16].reshape(128, 128).T.reshape(8, 2, 8, 128)
                folded = turned[:, 0] + turned[:, 1]
                folded = (folded[:, 0:4] + folded[:, 4:8]).reshape(32, 128)
                stage[k // 4, pl.ds(pl.multiple_of((k % 4) * 32, 32), 32), part * 128:(part + 1) * 128] = (
                    jnp.where(on > 0, folded, 0.0))
            return 0

        lax.fori_loop(0, count, finish, 0)

    for side in range(2):
        for part in range(2):
            out_ref[side, part * 128:(part + 1) * 128] = stage[side, :, part * 128:(part + 1) * 128].T


def score(position, pattern, plan, rows, dt):
    smem = pl.BlockSpec(memory_space=pltpu.SMEM)
    vmem = pl.BlockSpec(memory_space=pltpu.VMEM)
    return pl.pallas_call(
        functools.partial(score_kernel, position),
        name="score_blocks",
        out_shape=jax.ShapeDtypeStruct((2, 256, 128), jnp.float32),
        in_specs=[smem, smem, vmem, vmem],
        out_specs=vmem,
        scratch_shapes=[
            pltpu.VMEM((32, 4, 8, 256), jnp.float32),
            pltpu.VMEM((9, 32, 8, 128), jnp.float32),
            pltpu.VMEM((2, 128, 256), jnp.float32),
            pltpu.SMEM((8,), jnp.int32),
            pltpu.SMEM((8,), jnp.int32),
        ],
        compiler_params=pltpu.CompilerParams(vmem_limit_bytes=24 << 20),
    )(pattern, plan, rows, dt)


def swap_kernel(part_ref, meta_ref, out_ref, got, s_sem, r_sem):
    idx = lax.axis_index("docs")
    zh = lax.axis_index("pb")
    c, near = around(idx)
    twin = {"docs": idx + 1 - 2 * c, "pb": zh}
    partners = [{"docs": near[n][o], "pb": zh} for n in range(4) for o in range(2)]
    barrier = pltpu.get_barrier_semaphore()
    for d in partners + [twin]:
        pl.semaphore_signal(barrier, inc=1, device_id=d, device_id_type=MESH)
    pl.semaphore_wait(barrier, 9)
    copies = []
    for n in range(4):
        for o in range(2):
            q = 2 * n + o
            copies.append(pltpu.make_async_remote_copy(
                src_ref=part_ref.at[:, pl.ds(128 + 16 * q, 16)], dst_ref=got.at[c, :, pl.ds(64 + 16 * n, 16)],
                send_sem=s_sem.at[q], recv_sem=r_sem.at[q], device_id=partners[q], device_id_type=MESH))
    copies.append(pltpu.make_async_remote_copy(
        src_ref=part_ref.at[:, pl.ds(64, 64)], dst_ref=got.at[c, :, pl.ds(0, 64)],
        send_sem=s_sem.at[8], recv_sem=r_sem.at[8], device_id=twin, device_id_type=MESH))
    for cp in copies:
        cp.start()
    got[c, :, 0:64] = part_ref[:, 0:64]
    rank = jnp.broadcast_to(meta_ref[0, 1:2], (128, 128))
    for core, arrivals in ((c, copies[0:8:2]), (1 - c, copies[1:8:2] + copies[8:])):
        for cp in arrivals:
            cp.wait_recv()
        for half in range(2):
            back = jnp.take_along_axis(got[core, half].T, rank, axis=1).reshape(4, 8, 4, 128)
            for k in range(4):
                for h in range(8):
                    out_ref[(half * 4 + k) * 16 + h * 2 + core] = back[k, h]
    for cp in copies:
        cp.wait_send()


def swap(part, meta):
    vmem = pl.BlockSpec(memory_space=pltpu.VMEM)
    return pl.pallas_call(
        swap_kernel,
        name="swap_scores",
        out_shape=jax.ShapeDtypeStruct((128, 4, 128), jnp.float32),
        in_specs=[vmem, vmem],
        out_specs=vmem,
        scratch_shapes=[
            pltpu.VMEM((2, 2, 128, 128), jnp.float32),
            pltpu.SemaphoreType.DMA((9,)),
            pltpu.SemaphoreType.DMA((9,)),
        ],
        compiler_params=pltpu.CompilerParams(collective_id=1, has_side_effects=True, vmem_limit_bytes=4 << 20),
    )(part, meta)


def local(queries, documents, lengths, pattern):
    rows, dt, meta, plan = gather(queries, lengths.reshape(1, 128), documents, pattern)
    part = score(lambda: lax.axis_index("docs"), pattern, plan, rows.reshape(8, 8, 128, 128), dt)
    return swap(part, meta)


def solution(mesh):
    return jax.shard_map(
        local,
        mesh=mesh,
        in_specs=(P("docs", "pb", None), P("docs", None, None), P("docs"), P()),
        out_specs=P(None, "pb", "docs"),
        check_vma=False,
    )
```

```python
import functools

import jax
import jax.numpy as jnp
from jax import lax
from jax.experimental import pallas as pl
from jax.experimental.pallas import tpu as pltpu
from jax.sharding import PartitionSpec as P

MESH = pl.DeviceIdType.MESH
CH = 64
NS = 12
RUN = NS // 2


def device(y, zl, x, c, h):
    return {"docs": ((y * 4 + zl) * 4 + x) * 2 + c, "pb": h}


def around(idx):
    c, x, zl, y = idx % 2, (idx // 2) % 4, (idx // 8) % 4, idx // 32

    def at(y, x, c):
        return ((y * 4 + zl) * 4 + x) * 2 + c

    xp, xm, yp, ym = (x + 1) % 4, (x + 3) % 4, (y + 1) % 4, (y + 3) % 4
    return c, [[at(v, u, w) for w in (c, 1 - c)] for v, u in ((y, xm), (y, xp), (ym, x), (yp, x))]


def sides_of(idx):
    c, near = around(idx)
    sides = [(idx, 0, 8, 0, 0), (idx + 1 - 2 * c, 8, 8, 1, 0)]
    for n in range(4):
        for o in range(2):
            sides.append((near[n][o], 16 + 4 * n + 2 * o, 2, 2 + 2 * n + o, 8 + 2 * n))
    return sides


def list_steps(idx, tables, pattern, plan):
    row = lax.broadcasted_iota(jnp.int32, (32, 128), 0)
    lane = lax.broadcasted_iota(jnp.int32, (32, 128), 1)
    col = jnp.zeros((32, 128), jnp.int32)
    first = jnp.zeros((32, 128), jnp.int32)
    values = jnp.zeros((32, 128), jnp.int32)
    for block, here, groups, table, there in sides_of(idx):
        mine = (row >= here) & (row < here + groups)
        col = jnp.where(mine, block, col)
        first = jnp.where(mine, (there + row - here) * 8, first)
        values = jnp.where(mine, jnp.broadcast_to(tables[table, 3:4], (32, 128)), values)
    need = jnp.sum(jnp.where(lane == first, values, 0), axis=1, keepdims=True)
    t = lax.broadcasted_iota(jnp.int32, (32, 384), 1)
    for k in range(8):
        flags = jnp.broadcast_to(pattern[k:k + 1], (32, 128))
        on = jnp.sum(jnp.where(lane == col, flags, 0), axis=1, keepdims=True)
        size = jnp.where(on > 0, need, 0)
        turned = jnp.sum(jnp.where(lane == row, size, 0), axis=0, keepdims=True)
        ends = jnp.sum(jnp.where(lane <= row, turned, 0), axis=1, keepdims=True)
        steps = jnp.sum(turned, axis=1, keepdims=True)
        place = jnp.minimum(t, steps - 1)
        listed = place[0:1] + jnp.sum(jnp.where(ends <= place, 8 - size, 0), axis=0, keepdims=True)
        plan[k:k + 1, 0:384] = listed
        plan[k:k + 1, 384:512] = jnp.broadcast_to(steps, (1, 128))


SHARES = (0, 2, 4, 6, 9, 11, 13, 15, 1, 14, 3, 12, 5, 10, 7, 8)


def placed(rank):
    group = rank // 8
    slot = jnp.zeros_like(rank)
    for n, g in enumerate(SHARES):
        slot = jnp.where(group == g, n, slot)
    return slot * 8 + rank % 8


def gather_kernel(q_hbm, len_hbm, d_hbm, pat_hbm, q_out, dt_out, meta_out, plan_out,
                  q_ref, len_ref, pat_ref, tables, plan, tmp, prep, docs, wide, dt, meta, meta_s, zs, zr, ss, sr, ts, tr, ls):
    loads = [pltpu.make_async_copy(src, dst, ls.at[5 + n])
             for n, (src, dst) in enumerate(((q_hbm, q_ref), (len_hbm, len_ref), (d_hbm, docs), (pat_hbm, pat_ref)))]
    for cp in loads:
        cp.start()
    idx = lax.axis_index("docs")
    zh = lax.axis_index("pb")
    c = idx % 2
    x = (idx // 2) % 4
    zl = (idx // 8) % 4
    y = idx // 32
    z = zh * 4 + zl
    xp, xm, yp, ym = (x + 1) % 4, (x + 3) % 4, (y + 1) % 4, (y + 3) % 4
    x2, y2 = (x + 2) % 4, (y + 2) % 4
    right, left = device(y, zl, xp, c, zh), device(y, zl, xm, c, zh)
    up, down = device(yp, zl, x, c, zh), device(ym, zl, x, c, zh)
    twin = device(y, zl, x, 1 - c, zh)
    column = []
    for s in (4, 3, 5, 2, 6, 1, 7):
        zt = (z + s) % 8
        column.append((zt // 4, device(y, zt % 4, x, c, zt // 4)))

    barrier = pltpu.get_barrier_semaphore()
    for d in [d for _, d in column] + [right, left, up, down, twin]:
        pl.semaphore_signal(barrier, inc=1, device_id=d, device_id_type=MESH)

    loads[0].wait()
    for h in range(2):
        for q in range(4):
            tmp[pl.ds(q, 16, stride=4), :] = q_ref[4 * h + q].astype(jnp.float32)
        prep[h] = tmp[...].astype(jnp.bfloat16)

    loads[1].wait()
    lanes = jnp.broadcast_to(len_ref[...], (128, 128))
    cols = lanes.T
    r = lax.broadcasted_iota(jnp.int32, (128, 128), 0)
    k = lax.broadcasted_iota(jnp.int32, (128, 128), 1)
    ahead_col = (lanes > cols) | ((lanes == cols) & (k < r))
    ahead_row = (cols > lanes) | ((cols == lanes) & (r < k))
    rank_col = placed(jnp.sum(jnp.where(ahead_col, 1, 0), axis=1, keepdims=True))
    rank_row = placed(jnp.sum(jnp.where(ahead_row, 1, 0), axis=0, keepdims=True))
    here = rank_col == k
    sizes = jnp.sum(jnp.where(here, cols, 0), axis=0, keepdims=True)
    meta[0:1] = sizes
    meta[1:2] = rank_row
    meta[2:3] = jnp.sum(jnp.where(here, r, 0), axis=0, keepdims=True)
    meta[3:4] = (sizes + 7) // 8
    meta[4:8] = jnp.zeros((4, 128), jnp.int32)
    lm = pltpu.make_async_copy(meta, meta_s, ls.at[2])
    lm.start()
    lm.wait()
    share = []
    loads[2].wait()

    def arrange(g, _):
        for i in range(8):
            rows = docs[jnp.bitwise_and(meta_s[2, g * 8 + i], 127)].astype(jnp.float32)
            slot = lax.broadcasted_iota(jnp.int32, rows.shape, 0)
            wide[pl.ds(i, 64, stride=8), :] = jnp.where(slot < meta_s[0, g * 8 + i], rows, rows[0:1])
        for i in range(8):
            dt[g * 8 + i] = wide[i * CH:(i + 1) * CH].astype(jnp.bfloat16)
        return 0

    lax.fori_loop(8, 16, arrange, 0)
    pl.semaphore_wait(barrier, 12)

    own = q_out.at[y, zl, x, zh]
    waits = []

    def send(src, dst, s_sem, r_sem, d):
        cp = pltpu.make_async_remote_copy(
            src_ref=src, dst_ref=dst, send_sem=s_sem, recv_sem=r_sem, device_id=d, device_id_type=MESH)
        cp.start()
        waits.append(cp)
        return cp

    first = [send(prep.at[ht], own, zs.at[s], zr.at[s], d) for s, (ht, d) in enumerate(column)]
    lc = pltpu.make_async_copy(prep.at[zh], own, ls.at[1])
    lc.start()

    dests = (right, left, up, down)
    lo = pltpu.make_async_copy(meta, meta_out.at[0], ls.at[3])
    lo.start()
    m0 = send(meta, meta_out.at[1], ts.at[0], tr.at[0], twin)
    for n, d in enumerate(dests):
        share.append(send(meta, meta_out.at[2 + 2 * n], ts.at[6 + n], tr.at[6 + n], d))
    for n, d in enumerate(dests):
        share.append(send(dt.at[pl.ds(64 + 16 * n, 16)], dt_out.at[pl.ds(128 + 32 * n, 16)],
                          ts.at[2 + n], tr.at[2 + n], d))
    lax.fori_loop(0, 8, arrange, 0)
    ld = pltpu.make_async_copy(dt.at[pl.ds(0, 64)], dt_out.at[pl.ds(0, 64)], ls.at[4])
    ld.start()
    m1 = send(dt.at[pl.ds(0, 64)], dt_out.at[pl.ds(64, 64)], ts.at[1], tr.at[1], twin)

    lc.wait()
    for cp in first:
        cp.wait_recv()

    a = pl.ds(0, 2)
    b = pl.ds(2, 2)
    used = [0]

    def pass_on(ref, d):
        n = used[0]
        used[0] += 1
        return send(ref, ref, ss.at[n], sr.at[n], d)

    def spread_a(xs):
        return pass_on(q_out.at[y, a, xs], up), pass_on(q_out.at[y, a, xs], down)

    def spread_b(ys):
        return pass_on(q_out.at[ys, b, x], right), pass_on(q_out.at[ys, b, x], left)

    def relay_a(xs, pair):
        pair[0].wait_recv()
        f = pass_on(q_out.at[ym, 0, xs], up)
        pair[1].wait_recv()
        return f, pass_on(q_out.at[yp, 1, xs], down)

    def relay_b(ys, pair):
        pair[0].wait_recv()
        f = pass_on(q_out.at[ys, 2, xm], right)
        pair[1].wait_recv()
        return f, pass_on(q_out.at[ys, 3, xp], left)

    s0 = pass_on(q_out.at[y, a, x], right)
    s1 = pass_on(q_out.at[y, a, x], left)
    s2 = pass_on(q_out.at[y, b, x], up)
    s3 = pass_on(q_out.at[y, b, x], down)
    a0 = spread_a(x)
    b0 = spread_b(y)
    s0.wait_recv()
    s4 = pass_on(q_out.at[y, 0, xm], right)
    s1.wait_recv()
    s5 = pass_on(q_out.at[y, 1, xp], left)
    s2.wait_recv()
    s6 = pass_on(q_out.at[ym, 2, x], up)
    s3.wait_recv()
    s7 = pass_on(q_out.at[yp, 3, x], down)
    for n in range(4):
        share[n].wait_recv()
        m2 = meta_out.at[2 + 2 * n]
        share.append(send(m2, meta_out.at[3 + 2 * n], ts.at[14 + n], tr.at[14 + n], twin))
    a1 = spread_a(xm)
    a2 = spread_a(xp)
    b1 = spread_b(ym)
    b2 = spread_b(yp)
    early = list(relay_a(x, a0)) + list(relay_b(y, b0))
    s4.wait_recv()
    s5.wait_recv()
    a3 = spread_a(x2)
    s6.wait_recv()
    s7.wait_recv()
    b3 = spread_b(y2)
    last = early
    for xs, ys, pa, pb in ((xm, ym, a1, b1), (xp, yp, a2, b2), (x2, y2, a3, b3)):
        last.extend(relay_a(xs, pa))
        last.extend(relay_b(ys, pb))
        if xs is xm:
            for n in range(4):
                share[4 + n].wait_recv()
                share.append(send(dt_out.at[pl.ds(128 + 32 * n, 16)], dt_out.at[pl.ds(144 + 32 * n, 16)],
                                  ts.at[10 + n], tr.at[10 + n], twin))
    for cp in [m0] + share[8:12]:
        cp.wait_recv()
    lt = pltpu.make_async_copy(meta_out, tables, ls.at[9])
    lo.wait()
    lt.start()
    loads[3].wait()
    lt.wait()
    list_steps(idx, tables, pat_ref, plan)
    lp = pltpu.make_async_copy(plan, plan_out, ls.at[10])
    lp.start()
    for cp in [m1] + share[12:] + last:
        cp.wait_recv()
    for cp in (ld, lp):
        cp.wait()
    for cp in waits:
        cp.wait_send()


def gather(queries, lengths, documents, pattern):
    hbm = pl.BlockSpec(memory_space=pltpu.HBM)
    free = pl.BlockSpec(memory_space=pl.ANY)
    return pl.pallas_call(
        gather_kernel,
        name="gather_queries",
        out_shape=(
            jax.ShapeDtypeStruct((4, 4, 4, 2, 64, 128), jnp.bfloat16),
            jax.ShapeDtypeStruct((256, CH, 128), jnp.bfloat16),
            jax.ShapeDtypeStruct((10, 8, 128), jnp.int32),
            jax.ShapeDtypeStruct((8, 512), jnp.int32),
        ),
        in_specs=[hbm, hbm, hbm, hbm],
        out_specs=(free, free, free, free),
        scratch_shapes=[
            pltpu.VMEM((8, 16, 128), jnp.bfloat16),
            pltpu.VMEM((1, 128), jnp.int32),
            pltpu.VMEM((8, 128), jnp.int32),
            pltpu.VMEM((10, 8, 128), jnp.int32),
            pltpu.VMEM((8, 512), jnp.int32),
            pltpu.VMEM((64, 128), jnp.float32),
            pltpu.VMEM((2, 64, 128), jnp.bfloat16),
            pltpu.VMEM((128, 64, 128), jnp.bfloat16),
            pltpu.VMEM((512, 128), jnp.float32),
            pltpu.VMEM((128, CH, 128), jnp.bfloat16),
            pltpu.VMEM((8, 128), jnp.int32),
            pltpu.SMEM((8, 128), jnp.int32),
            pltpu.SemaphoreType.DMA((7,)),
            pltpu.SemaphoreType.DMA((7,)),
            pltpu.SemaphoreType.DMA((40,)),
            pltpu.SemaphoreType.DMA((40,)),
            pltpu.SemaphoreType.DMA((18,)),
            pltpu.SemaphoreType.DMA((18,)),
            pltpu.SemaphoreType.DMA((11,)),
        ],
        compiler_params=pltpu.CompilerParams(collective_id=0, has_side_effects=True, vmem_limit_bytes=12 << 20),
    )(*[pltpu.with_memory_space_constraint(v, pltpu.HBM) for v in (queries, lengths, documents, pattern)])


def score_kernel(position, *refs):
    pl.run_scoped(
        functools.partial(score_body, position, *refs),
        *([pltpu.ACC(0)((CH, 256), jnp.float32)] * NS + [pltpu.ACC(1)((CH, 256), jnp.float32)] * NS),
    )


def score_body(position, pat_ref, plan, rows, dt, out_ref, amax, total, stage, steps, blocks, *accs):
    acc = (accs[:NS], accs[NS:])
    sides = sides_of(position())

    def active(k, n):
        t = plan[k, 384]

        @pl.when(t > 0)
        def _():
            blocks[n] = k
            steps[n] = (t + RUN - 1) // RUN

        return n + (t > 0).astype(jnp.int32)

    count = lax.fori_loop(0, 8, active, jnp.int32(0))
    stage[...] = jnp.zeros_like(stage)

    def weights(p):
        k = blocks[p]
        for m in range(2):
            w = []
            for half in range(2):
                low = (2 * half + m) * 32
                w.append(jnp.concatenate([rows[k, :, low + 16 * t:low + 16 * t + 16, :].reshape(128, 128) for t in range(2)], axis=0))
            pltpu.matmul_push_rhs(jnp.concatenate(w, axis=1), 0, m, transpose=True)

    def push(at, s, head=False):
        w = dt[at]
        for half in range(2):
            v = [w, jnp.zeros_like(w)]
            v = jnp.concatenate(v[::-1] if half else v, axis=1)
            for m in range(2):
                if head and half == 0:
                    pltpu.matmul_acc_lhs(acc[m][2 * s], v, load_staged_rhs=0)
                else:
                    pltpu.matmul_acc_lhs(acc[m][2 * s + half], v)

    def pop(at, s, tops):
        g = jnp.right_shift(at, 3)
        roof = jnp.where(jnp.bitwise_and(at, 7) == 0, -jnp.inf, jnp.inf).astype(jnp.float32)
        after = []
        for half in range(2):
            for m in range(2):
                r = pltpu.matmul_pop(acc[m][2 * s + half])
                r = jnp.max(r.reshape(8, 8, 256), axis=0)
                r = jnp.maximum(jnp.minimum(tops[2 * half + m], roof), r)
                amax[g, 2 * half + m] = r
                after.append(r)
        return after

    def close(p):
        value = (amax[:, 0] + amax[:, 1]) + (amax[:, 2] + amax[:, 3])
        total[p] = value[:, :, :128] + value[:, :, 128:]

    @pl.when(count > 0)
    def _():
        weights(0)

        def one_block(p, state):
            p0, last0, tops = state
            n = steps[p]
            k, k0 = blocks[p], blocks[jnp.maximum(p0, 0)]
            olds = [plan[k0, last0 * RUN + s] for s in range(RUN)]
            news = [plan[k, s] for s in range(RUN)]
            for s in range(RUN):
                tops = pop(olds[s], s, tops)
                push(news[s], s, head=s == 0)
            weights(jnp.minimum(p + 1, count - 1))
            close(jnp.where(p0 < 0, 8, p0))

            def further(m, tops):
                olds = [plan[k, (m - 1) * RUN + s] for s in range(RUN)]
                news = [plan[k, m * RUN + s] for s in range(RUN)]
                for s in range(RUN):
                    tops = pop(olds[s], s, tops)
                    push(news[s], s)
                return tops

            return p, n - 1, lax.fori_loop(1, n, further, tops)

        zero = jnp.int32(0)
        start = [jnp.full((8, 256), -jnp.inf, jnp.float32)] * 4
        p, last, tops = lax.fori_loop(0, count, one_block, (zero - 1, zero, start))
        for s in range(RUN):
            tops = pop(plan[blocks[p], last * RUN + s], s, tops)
        close(p)
        push(0, 0, head=True)
        for half in range(2):
            for m in range(2):
                pltpu.matmul_pop(acc[m][half])

        lane = lax.broadcasted_iota(jnp.int32, (32, 128), 1)

        def finish(p, _):
            k = blocks[p]
            flags = [pat_ref[k, side[0]] for side in sides]
            for part in range(2):
                on = jnp.zeros((32, 128), jnp.int32)
                for flag, (_, here, groups, _, _) in zip(flags, sides):
                    if here // 16 == part:
                        low = (here % 16) * 8
                        on = jnp.where((lane >= low) & (lane < low + groups * 8), flag, on)
                turned = total[p, part * 16:(part + 1) * 16].reshape(128, 128).T.reshape(8, 2, 8, 128)
                folded = turned[:, 0] + turned[:, 1]
                folded = (folded[:, 0:4] + folded[:, 4:8]).reshape(32, 128)
                stage[k // 4, pl.ds(pl.multiple_of((k % 4) * 32, 32), 32), part * 128:(part + 1) * 128] = (
                    jnp.where(on > 0, folded, 0.0))
            return 0

        lax.fori_loop(0, count, finish, 0)

    for side in range(2):
        for part in range(2):
            out_ref[side, part * 128:(part + 1) * 128] = stage[side, :, part * 128:(part + 1) * 128].T


def score(position, pattern, plan, rows, dt):
    smem = pl.BlockSpec(memory_space=pltpu.SMEM)
    vmem = pl.BlockSpec(memory_space=pltpu.VMEM)
    return pl.pallas_call(
        functools.partial(score_kernel, position),
        name="score_blocks",
        out_shape=jax.ShapeDtypeStruct((2, 256, 128), jnp.float32),
        in_specs=[smem, smem, vmem, vmem],
        out_specs=vmem,
        scratch_shapes=[
            pltpu.VMEM((32, 4, 8, 256), jnp.float32),
            pltpu.VMEM((9, 32, 8, 128), jnp.float32),
            pltpu.VMEM((2, 128, 256), jnp.float32),
            pltpu.SMEM((8,), jnp.int32),
            pltpu.SMEM((8,), jnp.int32),
        ],
        compiler_params=pltpu.CompilerParams(vmem_limit_bytes=24 << 20),
    )(pattern, plan, rows, dt)


def swap_kernel(part_ref, meta_ref, out_ref, got, s_sem, r_sem):
    idx = lax.axis_index("docs")
    zh = lax.axis_index("pb")
    c, near = around(idx)
    twin = {"docs": idx + 1 - 2 * c, "pb": zh}
    partners = [{"docs": near[n][o], "pb": zh} for n in range(4) for o in range(2)]
    barrier = pltpu.get_barrier_semaphore()
    for d in partners + [twin]:
        pl.semaphore_signal(barrier, inc=1, device_id=d, device_id_type=MESH)
    pl.semaphore_wait(barrier, 9)
    copies = []
    for n in range(4):
        for o in range(2):
            q = 2 * n + o
            copies.append(pltpu.make_async_remote_copy(
                src_ref=part_ref.at[:, pl.ds(128 + 16 * q, 16)], dst_ref=got.at[c, :, pl.ds(64 + 16 * n, 16)],
                send_sem=s_sem.at[q], recv_sem=r_sem.at[q], device_id=partners[q], device_id_type=MESH))
    copies.append(pltpu.make_async_remote_copy(
        src_ref=part_ref.at[:, pl.ds(64, 64)], dst_ref=got.at[c, :, pl.ds(0, 64)],
        send_sem=s_sem.at[8], recv_sem=r_sem.at[8], device_id=twin, device_id_type=MESH))
    for cp in copies:
        cp.start()
    got[c, :, 0:64] = part_ref[:, 0:64]
    rank = jnp.broadcast_to(meta_ref[0, 1:2], (128, 128))
    for cp in copies:
        cp.wait_recv()
    for core in range(2):
        for half in range(2):
            back = jnp.take_along_axis(got[core, half].T, rank, axis=1).reshape(4, 8, 4, 128)
            for k in range(4):
                for h in range(8):
                    out_ref[(half * 4 + k) * 16 + h * 2 + core] = back[k, h]
    for cp in copies:
        cp.wait_send()


def swap(part, meta):
    vmem = pl.BlockSpec(memory_space=pltpu.VMEM)
    return pl.pallas_call(
        swap_kernel,
        name="swap_scores",
        out_shape=jax.ShapeDtypeStruct((128, 4, 128), jnp.float32),
        in_specs=[vmem, vmem],
        out_specs=vmem,
        scratch_shapes=[
            pltpu.VMEM((2, 2, 128, 128), jnp.float32),
            pltpu.SemaphoreType.DMA((9,)),
            pltpu.SemaphoreType.DMA((9,)),
        ],
        compiler_params=pltpu.CompilerParams(collective_id=1, has_side_effects=True, vmem_limit_bytes=4 << 20),
    )(part, meta)


def local(queries, documents, lengths, pattern):
    rows, dt, meta, plan = gather(queries, lengths.reshape(1, 128), documents, pattern)
    part = score(lambda: lax.axis_index("docs"), pattern, plan, rows.reshape(8, 8, 128, 128), dt)
    return swap(part, meta)


def solution(mesh):
    return jax.shard_map(
        local,
        mesh=mesh,
        in_specs=(P("docs", "pb", None), P("docs", None, None), P("docs"), P()),
        out_specs=P(None, "pb", "docs"),
        check_vma=False,
    )
```
